32 devices in a mesh: groups: 2 (over x), tile: 16 (over z, y, core).
Axes of the slice: x: 2, y: 2, z: 4, core: 2. Of those that a mesh axis runs over, the one named last changes fastest.
Arguments:
- start_model: float32 [2, 32768, 128], P(None, ('groups', 'tile')), parts along dimension 1, may hold values from -6 to 6
- v_basis: bfloat16 [2, 26624, 1024], P(None, ('groups', 'tile')), parts along dimension 1, may hold values from -0.125 to 0.125
- u_basis: bfloat16 [2, 1, 832, 32768], P(None, None, None, ('groups', 'tile')), parts along dimension 3, may hold values from -0.15625 to 0.15625
- records: bfloat16 [32, 128, 32768], P(None, None, ('groups', 'tile')), parts along dimension 2, may hold values from -6 to 6
- tile_ranks: int32 [2, 16, 16], P('groups'), parts along dimension 0, may hold values from 8 to 96, as said below
- window_start: int32 [128, 32768], P(None, ('groups', 'tile')), parts along dimension 1, may hold values from 0 to 7, as said below
- window_stop: int32 [128, 32768], P(None, ('groups', 'tile')), parts along dimension 1, may hold values from 16 to 31
Outputs:
- final_model: float32 [2, 32768, 128], P(None, ('groups', 'tile')), parts along dimension 1
The draws below stay inside these ranges and needn't reach their ends.
There are 2 independent parts, one for each index of `groups`. The reference program is written for one: setup_inputs(seed, part) draws one part's arguments, and reference() takes and returns one part's arrays. A program takes and returns all parts, laid end to end along the dimension named above; each array names one. Nothing has to cross between parts.
Inputs may be any that keep to these rules, and one draw needn't show every extreme that they name: `tile_ranks`: every tile row and every tile column of one frequency holds the same 16 ranks, each once, and they sum to 832; every frequency has tiles of rank 96 and of rank 8. window_stop - window_start lies between 16 and 24 for every pair.
All inputs are finite; a program needn't handle non-finite values.
Results may differ from the reference program's by a relative error of at most 0.012.
Values may be sent and summed in bfloat16 or wider, within the bound.
A program may use at most 128 MiB of HBM per device.

```python
import math
import jax
import jax.numpy as jnp
from jax import lax

NB = 1024
CT = 16
RT = 16
NVS = 128
RMIN = 8
RMAX = 96
NT = 32
ITERS = 2
F = 1
N = 16384
NR = 16384
RSUM = 832
PIECES = 1
PROWS = 1024


def permute_tiles(subkey):
    return jax.random.permutation(subkey, CT).astype(jnp.int32)


def rank_layout(key):
    half_count = CT // 2
    chosen = jax.random.randint(jax.random.fold_in(key, 11), (F, half_count), RMIN, RMAX + 1)
    leading = jnp.arange(half_count, dtype=jnp.int32)[None, :] == 0
    chosen = jnp.where(leading, RMAX, chosen)
    rank_values = jnp.concatenate([chosen, RMIN + RMAX - chosen], axis=1)
    row_keys = jax.random.split(jax.random.fold_in(key, 12), F)
    col_keys = jax.random.split(jax.random.fold_in(key, 13), F)
    row_order = jax.vmap(permute_tiles)(row_keys)
    col_order = jax.vmap(permute_tiles)(col_keys)
    position = (row_order[:, :, None] + col_order[:, None, :]) % CT
    spread = jnp.broadcast_to(rank_values[:, None, :], (F, RT, CT))
    return jnp.take_along_axis(spread, position, axis=2).astype(jnp.int32)


def window_layout(key):
    openings = jax.random.randint(jax.random.fold_in(key, 21), (NVS, NR), 0, NT // 4)
    spans = jax.random.randint(jax.random.fold_in(key, 22), (NVS, NR), NT // 2, 3 * NT // 4 + 1)
    return (openings.astype(jnp.int32), (openings + spans).astype(jnp.int32))


def draw_tile_ranks(key, part):
    return rank_layout(key)


def draw_window_start(key, part):
    return window_layout(key)[0]


def draw_window_stop(key, part):
    return window_layout(key)[1]


def block_levels(stream_key, shape, pieces, low, top_value):
    level = 1.0
    for dim, parts in pieces:
        heights = jax.random.uniform(jax.random.fold_in(jax.random.fold_in(stream_key, 6), dim), (parts,), jnp.float32, low / len(pieces), top_value / len(pieces))
        level = level * jnp.repeat(jnp.exp(heights), shape[dim] // parts).reshape((-1,) + (1,) * (len(shape) - 1 - dim))
    return level


def scatter_about(stream_key, extent, scale, reach, cuts=(), kind=jnp.bfloat16):
    factor_of = block_levels(stream_key, extent, cuts, -0.22, 0.18) if cuts else 1.0
    values = jax.random.normal(stream_key, extent, jnp.float32) * scale * factor_of
    return jnp.minimum(jnp.maximum(values, -reach), reach).astype(kind)


def setup_inputs(seed: int = 0, part: int = 0) -> dict:
    streams_of = jax.random.split(jax.random.key(seed), 8)
    own_keys = jax.random.split(jax.random.fold_in(streams_of[7], part), 8)
    start_model = scatter_about(own_keys[0], (2, F * N, NVS), 1.0, 6.0, ((1, 16),), jnp.float32)
    v_basis = scatter_about(own_keys[1], (2, F * CT * RSUM, NB), (2 * NB) ** -0.5, 0.125, ((1, 16),))
    u_basis = scatter_about(own_keys[2], (2, F, RSUM, NR), (2 * RSUM) ** -0.5, 0.15625, ((3, 16),))
    records = scatter_about(own_keys[3], (NT, NVS, NR), 1.0, 6.0, ((2, 16),))
    tile_ranks = draw_tile_ranks(jax.random.fold_in(jax.random.fold_in(streams_of[7], part), 71), part)
    window_start = draw_window_start(jax.random.fold_in(jax.random.fold_in(streams_of[7], part), 71), part)
    window_stop = draw_window_stop(jax.random.fold_in(jax.random.fold_in(streams_of[7], part), 71), part)
    return dict(start_model=start_model, v_basis=v_basis, u_basis=u_basis, records=records, tile_ranks=tile_ranks, window_start=window_start, window_stop=window_stop)


step_size = 0.5
precise = lax.Precision.HIGHEST

def wave_tables(bin_count, sample_count):
    moments = jnp.arange(sample_count, dtype=jnp.float32)
    bin_ids = jnp.arange(bin_count, dtype=jnp.float32) + 1.0
    phases = 2.0 * math.pi / sample_count * bin_ids[:, None] * moments[None, :]
    factor = math.sqrt(2.0 / sample_count)
    return (jnp.cos(phases) * factor, jnp.sin(phases) * factor)

def unpack_index(starts, slot_total):
    slot_ids = jnp.arange(slot_total, dtype=jnp.int32)
    owners = lax.optimization_barrier(jnp.sum((starts[..., None, :] <= slot_ids[:, None]).astype(jnp.int32), axis=-1)) - 1
    owner_start = jnp.take_along_axis(starts, owners, axis=-1)
    return (owners, slot_ids - owner_start)

def piece_tree(partials, axis):
    current = partials
    while current.shape[axis] > 1:
        half_count = current.shape[axis] // 2
        lower_part = lax.slice_in_dim(current, 0, half_count, axis=axis).astype(jnp.float32)
        upper_part = lax.slice_in_dim(current, half_count, 2 * half_count, axis=axis).astype(jnp.float32)
        current = lax.optimization_barrier((lower_part + upper_part).astype(jnp.bfloat16))
    return jnp.squeeze(current, axis)

def reference(start_model, v_basis, u_basis, records, tile_ranks, window_start, window_stop):
    down_offsets = jnp.cumsum(tile_ranks, axis=1) - tile_ranks
    side_offsets = jnp.cumsum(tile_ranks, axis=2) - tile_ranks
    col_owner, col_slot = unpack_index(side_offsets, RSUM)
    gather_u = (col_owner * RSUM + jnp.take_along_axis(down_offsets, col_owner, axis=2) + col_slot).astype(jnp.int32)
    down_swap = jnp.transpose(down_offsets, (0, 2, 1))
    side_swap = jnp.transpose(side_offsets, (0, 2, 1))
    row_owner, row_slot = unpack_index(down_swap, RSUM)
    gather_v = (row_owner * RSUM + jnp.take_along_axis(side_swap, row_owner, axis=2) + row_slot).astype(jnp.int32)
    v_blocks = jnp.transpose(v_basis.reshape(2, F, CT, RSUM, NB), (1, 0, 2, 3, 4))
    u_blocks = jnp.transpose(u_basis, (1, 0, 2, 3))
    cos_table, sin_table = wave_tables(F, NT)

    def forward_one(operands):
        v_freq, x_freq, u_freq, gather_ids = operands
        v_wide = v_freq.astype(jnp.float32)
        coeff_real = jnp.einsum('jkn,jns->jks', v_wide[0], x_freq[0]) - jnp.einsum('jkn,jns->jks', v_wide[1], x_freq[1])
        coeff_imag = jnp.einsum('jkn,jns->jks', v_wide[0], x_freq[1]) + jnp.einsum('jkn,jns->jks', v_wide[1], x_freq[0])
        packed = lax.optimization_barrier(jnp.stack([coeff_real, coeff_imag]).astype(jnp.bfloat16))
        packed = packed.astype(jnp.float32).reshape(2, CT * RSUM, NVS)
        chosen = packed[:, gather_ids]
        u_wide = u_freq.astype(jnp.float32).reshape(2, RSUM, RT, NB)
        pred_real = jnp.einsum('iks,kin->sin', chosen[0], u_wide[0]) - jnp.einsum('iks,kin->sin', chosen[1], u_wide[1])
        pred_imag = jnp.einsum('iks,kin->sin', chosen[0], u_wide[1]) + jnp.einsum('iks,kin->sin', chosen[1], u_wide[0])
        return jnp.stack([pred_real, pred_imag]).reshape(2, NVS, NR)

    def misfit_block(operands):
        pred_block, record_block, open_block, close_block = operands
        traces = jnp.einsum('ft,fsn->tsn', cos_table, pred_block[:, 0], precision=precise) - jnp.einsum('ft,fsn->tsn', sin_table, pred_block[:, 1], precision=precise)
        moments = jnp.arange(NT, dtype=jnp.int32)[:, None, None]
        inside = (moments >= open_block[None]) & (moments < close_block[None])
        residual = jnp.where(inside, traces - record_block.astype(jnp.float32), jnp.zeros((), jnp.float32))
        back_real = jnp.einsum('ft,tsn->fsn', cos_table, residual, precision=precise)
        back_imag = -jnp.einsum('ft,tsn->fsn', sin_table, residual, precision=precise)
        return jnp.stack([back_real, back_imag], axis=1).astype(jnp.bfloat16)

    def adjoint_one(operands):
        u_freq, back_freq, v_freq, gather_ids = operands
        u_wide = u_freq.astype(jnp.float32).reshape(2, RSUM, RT, PIECES, PROWS)
        back_wide = back_freq.astype(jnp.float32).reshape(2, NVS, RT, PIECES, PROWS)
        part_real = jnp.einsum('kipn,sipn->ipks', u_wide[0], back_wide[0]) + jnp.einsum('kipn,sipn->ipks', u_wide[1], back_wide[1])
        part_imag = jnp.einsum('kipn,sipn->ipks', u_wide[0], back_wide[1]) - jnp.einsum('kipn,sipn->ipks', u_wide[1], back_wide[0])
        partials = lax.optimization_barrier(jnp.stack([part_real, part_imag]).astype(jnp.bfloat16))
        summed = piece_tree(partials, 2)
        summed = summed.astype(jnp.float32).reshape(2, RT * RSUM, NVS)
        chosen = summed[:, gather_ids]
        v_wide = v_freq.astype(jnp.float32)
        grad_real = jnp.einsum('jkn,jks->jns', v_wide[0], chosen[0]) + jnp.einsum('jkn,jks->jns', v_wide[1], chosen[1])
        grad_imag = jnp.einsum('jkn,jks->jns', v_wide[0], chosen[1]) - jnp.einsum('jkn,jks->jns', v_wide[1], chosen[0])
        return jnp.stack([grad_real, grad_imag])
    record_blocks = jnp.transpose(records.reshape(NT, NVS, RT, NB), (2, 0, 1, 3))
    open_blocks = jnp.transpose(window_start.reshape(NVS, RT, NB), (1, 0, 2))
    close_blocks = jnp.transpose(window_stop.reshape(NVS, RT, NB), (1, 0, 2))
    current = start_model
    for iteration in range(ITERS):
        rounded = lax.optimization_barrier(current.astype(jnp.bfloat16)).astype(jnp.float32)
        x_blocks = jnp.transpose(rounded.reshape(2, F, CT, NB, NVS), (1, 0, 2, 3, 4))
        predicted = lax.map(forward_one, (v_blocks, x_blocks, u_blocks, gather_u))
        pred_blocks = jnp.transpose(predicted.reshape(F, 2, NVS, RT, NB), (3, 0, 1, 2, 4))
        back_blocks = lax.map(misfit_block, (pred_blocks, record_blocks, open_blocks, close_blocks))
        backward = jnp.transpose(back_blocks, (1, 2, 3, 0, 4)).reshape(F, 2, NVS, NR)
        gradient = lax.map(adjoint_one, (u_blocks, backward, v_blocks, gather_v))
        gradient = jnp.transpose(gradient, (1, 0, 2, 3, 4)).reshape(2, F * N, NVS)
        current = current - step_size * gradient
    return current
```

```python
import functools
import math

import jax
import jax.numpy as jnp
from jax import lax
from jax.experimental import pallas as pl
from jax.experimental.pallas import tpu as pltpu
from jax.sharding import PartitionSpec as P

RMAX = 96
ITERS = 2


step_size = 0.5
precise = lax.Precision.HIGHEST


def wave_tables(bin_count, sample_count):
    moments = jnp.arange(sample_count, dtype=jnp.float32)
    bin_ids = jnp.arange(bin_count, dtype=jnp.float32) + 1.0
    phases = 2.0 * math.pi / sample_count * bin_ids[:, None] * moments[None, :]
    factor = math.sqrt(2.0 / sample_count)
    return (jnp.cos(phases) * factor, jnp.sin(phases) * factor)


def piece_tree(partials, axis):
    current = partials
    while current.shape[axis] > 1:
        half_count = current.shape[axis] // 2
        lower_part = lax.slice_in_dim(current, 0, half_count, axis=axis).astype(jnp.float32)
        upper_part = lax.slice_in_dim(current, half_count, 2 * half_count, axis=axis).astype(
            jnp.float32
        )
        current = (lower_part + upper_part).astype(jnp.bfloat16)
    return jnp.squeeze(current, axis)


def starts_along(tile_ranks, axis):
    count = tile_ranks.shape[axis]
    return jnp.concatenate(
        [
            jnp.sum(lax.slice_in_dim(tile_ranks, 0, k, axis=axis), axis=axis, keepdims=True)
            for k in range(count)
        ],
        axis=axis,
    ).astype(jnp.int32)


def pack_slots(source_rows, rank_each, start_each):
    padded = jnp.pad(source_rows, ((0, 0), (0, RMAX), (0, 0)))
    live = jnp.arange(RMAX, dtype=jnp.int32)[None, :, None]

    def cut(operands):
        rank, start = operands
        rows = lax.dynamic_slice_in_dim(padded, start, RMAX, axis=1)
        return jnp.where(live < rank, rows, jnp.zeros((), rows.dtype))

    return jnp.moveaxis(lax.map(cut, (rank_each, start_each)), 0, 1)


def join_slots(slots, starts, total):
    joined = jnp.zeros((slots.shape[0], total + RMAX, slots.shape[3]), slots.dtype)

    def place(k, joined):
        rows = lax.dynamic_index_in_dim(slots, k, 1, False)
        return lax.dynamic_update_slice_in_dim(joined, rows, starts[k], axis=1)

    return lax.fori_loop(0, slots.shape[1], place, joined)[:, :total]


def on_device_general(start_model, v_basis, u_basis, records, tile_ranks, window_start, window_stop):
    tile_count = lax.axis_size("tile")
    device = lax.axis_index("tile")
    freq_count, rows_count, cols_count = tile_ranks.shape
    rank_total = v_basis.shape[1]
    pieces = tile_count // rows_count
    my_freq = device // cols_count
    my_col = device % cols_count
    my_row = device // pieces
    down_offsets = starts_along(tile_ranks, 1)
    side_offsets = starts_along(tile_ranks, 2)
    column_ranks = lax.dynamic_index_in_dim(
        lax.dynamic_index_in_dim(tile_ranks, my_freq, 0, False), my_col, 1, False
    )
    column_starts = lax.dynamic_index_in_dim(
        lax.dynamic_index_in_dim(down_offsets, my_freq, 0, False), my_col, 1, False
    )
    row_ranks = lax.dynamic_index_in_dim(tile_ranks, my_row, 1, False)
    row_starts = lax.dynamic_index_in_dim(side_offsets, my_row, 1, False)
    fwd_rank = jnp.broadcast_to(column_ranks[:, None], (rows_count, pieces)).reshape(tile_count)
    fwd_start = jnp.broadcast_to(column_starts[:, None], (rows_count, pieces)).reshape(tile_count)
    dest_freq = jnp.arange(tile_count, dtype=jnp.int32) // cols_count
    adj_rank = row_ranks.reshape(tile_count)
    adj_start = row_starts.reshape(tile_count) + dest_freq * rank_total
    cos_table, sin_table = wave_tables(freq_count, records.shape[0])
    moments = jnp.arange(records.shape[0], dtype=jnp.int32)[:, None, None]
    inside = (moments >= window_start[None]) & (moments < window_stop[None])
    observed = records.astype(jnp.float32)
    current = start_model
    for iteration in range(ITERS):
        rounded = current.astype(jnp.bfloat16)
        coeff_real = jnp.dot(v_basis[0], rounded[0], preferred_element_type=jnp.float32) - jnp.dot(
            v_basis[1], rounded[1], preferred_element_type=jnp.float32
        )
        coeff_imag = jnp.dot(v_basis[0], rounded[1], preferred_element_type=jnp.float32) + jnp.dot(
            v_basis[1], rounded[0], preferred_element_type=jnp.float32
        )
        coefficients = jnp.stack([coeff_real, coeff_imag]).astype(jnp.bfloat16)
        outbound = pack_slots(coefficients, fwd_rank, fwd_start)
        forward_received = lax.all_to_all(outbound, "tile", split_axis=1, concat_axis=1, tiled=True)
        grouped_cols = forward_received.reshape(
            2, freq_count, cols_count, RMAX, forward_received.shape[3]
        )
        forward_chosen = jnp.stack(
            [join_slots(grouped_cols[:, f], row_starts[f], rank_total) for f in range(freq_count)],
            axis=1,
        )
        pred_real = jnp.einsum(
            "fks,fkn->fsn", forward_chosen[0], u_basis[0], preferred_element_type=jnp.float32
        ) - jnp.einsum(
            "fks,fkn->fsn", forward_chosen[1], u_basis[1], preferred_element_type=jnp.float32
        )
        pred_imag = jnp.einsum(
            "fks,fkn->fsn", forward_chosen[0], u_basis[1], preferred_element_type=jnp.float32
        ) + jnp.einsum(
            "fks,fkn->fsn", forward_chosen[1], u_basis[0], preferred_element_type=jnp.float32
        )
        predicted = jnp.stack([pred_real, pred_imag])
        traces = jnp.einsum("ft,fsn->tsn", cos_table, predicted[0], precision=precise) - jnp.einsum(
            "ft,fsn->tsn", sin_table, predicted[1], precision=precise
        )
        residual = jnp.where(inside, traces - observed, jnp.zeros((), jnp.float32))
        back_real = jnp.einsum("ft,tsn->fsn", cos_table, residual, precision=precise)
        back_imag = -jnp.einsum("ft,tsn->fsn", sin_table, residual, precision=precise)
        adjoint_field = jnp.stack([back_real, back_imag]).astype(jnp.bfloat16)
        part_real = jnp.einsum(
            "fkn,fsn->fks", u_basis[0], adjoint_field[0], preferred_element_type=jnp.float32
        ) + jnp.einsum(
            "fkn,fsn->fks", u_basis[1], adjoint_field[1], preferred_element_type=jnp.float32
        )
        part_imag = jnp.einsum(
            "fkn,fsn->fks", u_basis[0], adjoint_field[1], preferred_element_type=jnp.float32
        ) - jnp.einsum(
            "fkn,fsn->fks", u_basis[1], adjoint_field[0], preferred_element_type=jnp.float32
        )
        partial_value = jnp.stack([part_real, part_imag]).astype(jnp.bfloat16)
        flat_partial = partial_value.reshape(2, freq_count * rank_total, partial_value.shape[3])
        outgoing = pack_slots(flat_partial, adj_rank, adj_start)
        received = lax.all_to_all(outgoing, "tile", split_axis=1, concat_axis=1, tiled=True)
        grouped_rows = received.reshape(2, rows_count, pieces, RMAX, received.shape[3])
        adjoint_summed = piece_tree(grouped_rows, 2)
        chosen = join_slots(adjoint_summed, column_starts, rank_total)
        contract_dims = (((0,), (0,)), ((), ()))
        grad_real = lax.dot_general(
            v_basis[0], chosen[0], contract_dims, preferred_element_type=jnp.float32
        ) + lax.dot_general(
            v_basis[1], chosen[1], contract_dims, preferred_element_type=jnp.float32
        )
        grad_imag = lax.dot_general(
            v_basis[0], chosen[1], contract_dims, preferred_element_type=jnp.float32
        ) - lax.dot_general(
            v_basis[1], chosen[0], contract_dims, preferred_element_type=jnp.float32
        )
        gradient = jnp.stack([grad_real, grad_imag])
        current = current - step_size * gradient
    return current


LANES = 128
CHUNKS = 4
PARTS = 2
f32 = jnp.float32
bf16 = jnp.bfloat16
far = pl.BlockSpec(memory_space=pltpu.HBM)
scalars = pl.BlockSpec(memory_space=pltpu.SMEM)


def dot_last(a, b):
    return lax.dot_general(a, b, (((1,), (1,)), ((), ())), preferred_element_type=f32)


def dot_first(a, b):
    return lax.dot_general(a, b, (((0,), (0,)), ((), ())), preferred_element_type=f32)


def xor_peer(me, mask, n):
    peer = me
    bit = 1
    while bit < n:
        if mask & bit:
            peer = peer + bit * (1 - 2 * ((me // bit) % 2))
        bit *= 2
    return peer


def add_windows(record_ref, open_ref, close_ref, sums_ref, first, count):
    sample_count = record_ref.shape[0]
    scale = math.sqrt(2.0 / sample_count)
    step, strip = 16, 4 * LANES
    strips = record_ref.shape[2] // strip

    def block(k, carry):
        rows = pl.ds(pl.multiple_of(first + (k // strips) * step, step), step)
        lanes = pl.ds(pl.multiple_of((k % strips) * strip, strip), strip)
        opened = open_ref[rows, lanes]
        closed = close_ref[rows, lanes]
        sums = [jnp.zeros(opened.shape, f32)] * 5
        for t in range(sample_count - 1):
            phase = 2.0 * math.pi / sample_count * t
            c, s = math.cos(phase) * scale, math.sin(phase) * scale
            seen = record_ref[t, rows, lanes].astype(f32)
            squares = (c * c, c * s, s * s)
            if sample_count // 4 <= t < sample_count // 2:
                terms = list(squares)
            else:
                inside = (t >= opened) if t < sample_count // 4 else (t < closed)
                seen = jnp.where(inside, seen, 0.0)
                terms = [jnp.where(inside, w, 0.0) for w in squares]
            terms += [seen * c, seen * s]
            sums = [x + y for x, y in zip(sums, terms)]
        for m in range(5):
            sums_ref[m, rows, lanes] = sums[m]
        return carry

    lax.fori_loop(0, (count // step) * strips, block, 0)


def fused_kernel(
    n, rank_ref, x_hbm, v_hbm, u_hbm, record_hbm, open_hbm, close_hbm, out_ref,
    x_ref, v_ref, u_ref, record_ref, open_ref, close_ref,
    xw_ref, xt_ref, sums_ref, rows_ref, slots_ref, joined_ref, send_ref, recv_ref,
    start_ref, table_ref, load_sem, v_sem, send_sem, recv_sem,
):
    me = lax.axis_index("tile")
    masks = list(range(n - 1, 0, -1))
    peers = [xor_peer(me, mask, n) for mask in masks]
    _, total, width = v_ref.shape
    sources = x_ref.shape[2]
    half = sources // 2
    batches = 2
    blocks = total // 8

    loads = [
        pltpu.make_async_copy(source, target, load_sem.at[k])
        for k, (source, target) in enumerate(
            [
                (x_hbm, x_ref),
                (open_hbm, open_ref),
                (close_hbm, close_ref),
                (record_hbm, record_ref),
                (u_hbm, u_ref),
            ]
        )
    ]
    part = total // CHUNKS
    v_loads = [
        pltpu.make_async_copy(
            v_hbm.at[:, pl.ds(k * part, part)], v_ref.at[:, pl.ds(k * part, part)], v_sem.at[k]
        )
        for k in range(CHUNKS)
    ]
    loads[0].start()
    for load in v_loads:
        load.start()
    for load in loads[1:]:
        load.start()

    barrier = pltpu.get_barrier_semaphore()
    for peer in peers:
        pl.semaphore_signal(
            barrier, inc=1, device_id={"tile": peer}, device_id_type=pl.DeviceIdType.MESH
        )

    row_start, column_start = 0, 0
    for k in range(n):
        start_ref[0, k] = row_start
        start_ref[1, k] = column_start
        row_start = row_start + rank_ref[me, k]
        column_start = column_start + rank_ref[k, me]
    for b in range(batches):
        rows_ref[b, pl.ds(total, RMAX), :] = jnp.zeros((RMAX, LANES), f32)

    def copy_of(e, b, d):
        return pltpu.make_async_remote_copy(
            src_ref=send_ref.at[e, b, d],
            dst_ref=recv_ref.at[e, b, me],
            send_sem=send_sem.at[e, b, d],
            recv_sem=recv_sem.at[e, b, d],
            device_id={"tile": peers[d]},
            device_id_type=pl.DeviceIdType.MESH,
        )

    def send_rows(e, b, side):
        def slot(k):
            return rows_ref[b, pl.ds(start_ref[side, k], RMAX), :].astype(bf16)

        for d, peer in enumerate(peers):
            send_ref[e, b, d] = slot(peer)
            copy_of(e, b, d).start()
        recv_ref[e, b, me] = slot(me)

    def join(e, b, side):
        for d in range(n - 1):
            copy_of(e, b, d).wait_recv()
        for k in range(n):
            slots_ref[pl.ds(k * RMAX, RMAX), :] = recv_ref[e, b, k].astype(f32)
        row = lax.broadcasted_iota(jnp.int32, (8, LANES), 0)

        def group(k):
            first = slots_ref[pl.ds(table_ref[side, 0, k], 8), :]
            second = slots_ref[pl.ds(table_ref[side, 1, k], 8), :]
            return jnp.where(row < table_ref[side, 2, k], first, second)

        for k in range(0, blocks, 2):
            pair = jnp.concatenate([group(k), group(k + 1)], axis=0)
            joined_ref[pl.ds(k * 8, 16), :] = pair.astype(bf16)

    lane = lax.broadcasted_iota(jnp.int32, (width, sources), 1)
    loads[0].wait()
    xr, xi = x_ref[0], x_ref[1]
    turned_r, turned_i = pltpu.roll(xr, half, 1), pltpu.roll(xi, half, 1)
    low = lane < half
    xw_ref[0, :, :sources] = jnp.where(low, xr, turned_i).astype(bf16)
    xw_ref[0, :, sources:] = jnp.where(low, turned_r, xi).astype(bf16)
    xw_ref[1, :, :sources] = jnp.where(low, -xi, turned_r).astype(bf16)
    xw_ref[1, :, sources:] = jnp.where(low, -turned_i, xr).astype(bf16)
    for k in range(CHUNKS):
        v_loads[k].wait()
        rows = pl.ds(k * part, part)
        value = jnp.dot(v_ref[0, rows, :], xw_ref[0], preferred_element_type=f32) + jnp.dot(
            v_ref[1, rows, :], xw_ref[1], preferred_element_type=f32
        )
        rows_ref[0, rows, :] = value[:, :LANES]
        rows_ref[1, rows, :] = value[:, LANES:]
    pl.semaphore_wait(barrier, n - 1)
    for b in range(batches):
        send_rows(0, b, 1)

    for side in range(2):

        def entry(k, carry):
            tile, start = carry
            end = start + (rank_ref[me, tile] if side == 0 else rank_ref[tile, me])
            table_ref[side, 0, k] = jnp.clip(tile * RMAX + k * 8 - start, 0, n * RMAX)
            table_ref[side, 1, k] = jnp.clip((tile + 1) * RMAX + k * 8 - end, 0, n * RMAX)
            table_ref[side, 2, k] = end - k * 8
            leave = end <= k * 8 + 8
            later = jnp.minimum(tile + 1, n - 1)
            return jnp.where(leave, later, tile), jnp.where(leave, end, start)

        lax.fori_loop(0, blocks, entry, (jnp.int32(0), jnp.int32(0)))
    slots_ref[pl.ds(n * RMAX, 8), :] = jnp.zeros((8, LANES), f32)
    for p in range(2):
        turned = x_ref[p].T
        for b in range(batches):
            xt_ref[b, pl.ds(p * half, half), :] = turned[b * half : (b + 1) * half]
    for load in loads[1:]:
        load.wait()

    def field_of(b):
        c = joined_ref[...]
        p = dot_first(c, u_ref[0])
        q = dot_first(c, u_ref[1])
        yr = p[:half] - q[half:]
        yi = q[:half] + p[half:]
        rows = pl.ds(pl.multiple_of(b * half, half), half)
        hr = sums_ref[0, rows, :] * yr - sums_ref[1, rows, :] * yi - sums_ref[3, rows, :]
        hi = sums_ref[2, rows, :] * yi - sums_ref[1, rows, :] * yr + sums_ref[4, rows, :]
        return hr.astype(bf16), hi.astype(bf16)

    def step_model(b):
        a = joined_ref[...]
        p = dot_first(a, v_ref[0])
        q = dot_first(a, v_ref[1])
        xr = xt_ref[b, :half, :] - step_size * (p[:half] + q[half:])
        xi = xt_ref[b, half:, :] - step_size * (p[half:] - q[:half])
        return xr, xi

    for iteration in range(ITERS):
        e = 2 * iteration

        def residual_step(b, carry):
            if iteration == 0:
                first = b * half
                add_windows(record_ref, open_ref, close_ref, sums_ref, first, half)
            join(e, b, 0)
            hr, hi = field_of(b)
            rows_ref[b, pl.ds(0, total), :] = dot_last(
                u_ref[0], jnp.concatenate([hr, hi], axis=0)
            ) + dot_last(u_ref[1], jnp.concatenate([hi, -hr], axis=0))
            send_rows(e + 1, b, 0)
            return carry

        lax.fori_loop(0, batches, residual_step, 0)
        if iteration + 1 < ITERS:

            def model_step(b, carry):
                join(e + 1, b, 1)
                xr, xi = step_model(b)
                xt_ref[b, :half, :] = xr
                xt_ref[b, half:, :] = xi
                xr, xi = xr.astype(bf16), xi.astype(bf16)
                rows_ref[b, pl.ds(0, total), :] = dot_last(
                    v_ref[0], jnp.concatenate([xr, xi], axis=0)
                ) + dot_last(v_ref[1], jnp.concatenate([-xi, xr], axis=0))
                send_rows(e + 2, b, 1)
                return carry

            lax.fori_loop(0, batches, model_step, 0)
        else:
            for b in range(batches):
                join(e + 1, b, 1)
                xr, xi = step_model(b)
                lanes = pl.ds(b * half, half)
                out_ref[0, :, lanes] = xr.T
                out_ref[1, :, lanes] = xi.T

    def finish(e, carry):
        for b in range(batches):
            for d in range(n - 1):
                copy_of(e, b, d).wait_send()
        return carry

    lax.fori_loop(0, 2 * ITERS, finish, 0)


def fused(start_model, v_basis, u_parts, records, ranks, window_start, window_stop):
    n = ranks.shape[0]
    _, width, sources = start_model.shape
    _, total, _ = v_basis.shape
    receivers = records.shape[2]
    exchanges, batches = 2 * ITERS, 2
    like = lambda a: pltpu.VMEM(a.shape, a.dtype)
    return pl.pallas_call(
        functools.partial(fused_kernel, n),
        out_shape=jax.ShapeDtypeStruct(start_model.shape, f32),
        in_specs=[scalars] + [far] * 6,
        out_specs=pl.BlockSpec(memory_space=pltpu.VMEM),
        scratch_shapes=[
            like(start_model),
            like(v_basis),
            like(u_parts),
            like(records),
            like(window_start),
            like(window_stop),
            pltpu.VMEM((2, width, 2 * sources), bf16),
            pltpu.VMEM((batches, sources, width), f32),
            pltpu.VMEM((5, sources, receivers), f32),
            pltpu.VMEM((batches, total + RMAX, LANES), f32),
            pltpu.VMEM((n * RMAX + 8, LANES), f32),
            pltpu.VMEM((total, LANES), bf16),
            pltpu.VMEM((exchanges, batches, n - 1, RMAX, LANES), bf16),
            pltpu.VMEM((exchanges, batches, n, RMAX, LANES), bf16),
            pltpu.SMEM((2, n), jnp.int32),
            pltpu.SMEM((2, 3, total // 8), jnp.int32),
            pltpu.SemaphoreType.DMA((5,)),
            pltpu.SemaphoreType.DMA((CHUNKS,)),
            pltpu.SemaphoreType.DMA((exchanges, batches, n - 1)),
            pltpu.SemaphoreType.DMA((exchanges, batches, n - 1)),
        ],
        compiler_params=pltpu.CompilerParams(
            collective_id=0, has_side_effects=True, vmem_limit_bytes=62 * 1024 * 1024
        ),
    )(ranks, start_model, v_basis, u_parts, records, window_start, window_stop)


def copy_kernel(source_ref, target_ref):
    target_ref[...] = source_ref[...]


def hand_over(model):
    parts, rows, lanes = model.shape
    block = pl.BlockSpec((parts, rows // PARTS, lanes), lambda k: (0, k, 0))
    return pl.pallas_call(
        copy_kernel,
        grid=(PARTS,),
        out_shape=jax.ShapeDtypeStruct(model.shape, model.dtype),
        in_specs=[block],
        out_specs=block,
    )(model)


def on_device(start_model, v_basis, u_basis, records, tile_ranks, window_start, window_stop):
    n = lax.axis_size("tile")
    freq_count, rows_count, cols_count = tile_ranks.shape
    single = freq_count == 1 and n == rows_count and n == cols_count and n & (n - 1) == 0
    fits = start_model.shape[2] == LANES and v_basis.shape[1] % (16 * CHUNKS) == 0
    fits = fits and records.shape[2] % (4 * LANES) == 0 and start_model.shape[1] % LANES == 0
    if not (single and fits):
        return on_device_general(
            start_model, v_basis, u_basis, records, tile_ranks, window_start, window_stop
        )
    final = fused(
        start_model, v_basis, u_basis[:, 0], records, tile_ranks[0], window_start, window_stop
    )
    return hand_over(final)


def solution(mesh):
    in_specs = (
        P(None, ("groups", "tile"), None),
        P(None, ("groups", "tile"), None),
        P(None, None, None, ("groups", "tile")),
        P(None, None, ("groups", "tile")),
        P("groups", None, None),
        P(None, ("groups", "tile")),
        P(None, ("groups", "tile")),
    )
    out_specs = P(None, ("groups", "tile"), None)
    return jax.shard_map(
        on_device, mesh=mesh, in_specs=in_specs, out_specs=out_specs, check_vma=False
    )
```

```python
import functools
import math

import jax
import jax.numpy as jnp
from jax import lax
from jax.experimental import pallas as pl
from jax.experimental.pallas import tpu as pltpu
from jax.sharding import PartitionSpec as P

RMAX = 96
ITERS = 2


step_size = 0.5
precise = lax.Precision.HIGHEST


def wave_tables(bin_count, sample_count):
    moments = jnp.arange(sample_count, dtype=jnp.float32)
    bin_ids = jnp.arange(bin_count, dtype=jnp.float32) + 1.0
    phases = 2.0 * math.pi / sample_count * bin_ids[:, None] * moments[None, :]
    factor = math.sqrt(2.0 / sample_count)
    return (jnp.cos(phases) * factor, jnp.sin(phases) * factor)


def piece_tree(partials, axis):
    current = partials
    while current.shape[axis] > 1:
        half_count = current.shape[axis] // 2
        lower_part = lax.slice_in_dim(current, 0, half_count, axis=axis).astype(jnp.float32)
        upper_part = lax.slice_in_dim(current, half_count, 2 * half_count, axis=axis).astype(
            jnp.float32
        )
        current = (lower_part + upper_part).astype(jnp.bfloat16)
    return jnp.squeeze(current, axis)


def starts_along(tile_ranks, axis):
    count = tile_ranks.shape[axis]
    return jnp.concatenate(
        [
            jnp.sum(lax.slice_in_dim(tile_ranks, 0, k, axis=axis), axis=axis, keepdims=True)
            for k in range(count)
        ],
        axis=axis,
    ).astype(jnp.int32)


def pack_slots(source_rows, rank_each, start_each):
    padded = jnp.pad(source_rows, ((0, 0), (0, RMAX), (0, 0)))
    live = jnp.arange(RMAX, dtype=jnp.int32)[None, :, None]

    def cut(operands):
        rank, start = operands
        rows = lax.dynamic_slice_in_dim(padded, start, RMAX, axis=1)
        return jnp.where(live < rank, rows, jnp.zeros((), rows.dtype))

    return jnp.moveaxis(lax.map(cut, (rank_each, start_each)), 0, 1)


def join_slots(slots, starts, total):
    joined = jnp.zeros((slots.shape[0], total + RMAX, slots.shape[3]), slots.dtype)

    def place(k, joined):
        rows = lax.dynamic_index_in_dim(slots, k, 1, False)
        return lax.dynamic_update_slice_in_dim(joined, rows, starts[k], axis=1)

    return lax.fori_loop(0, slots.shape[1], place, joined)[:, :total]


def on_device_general(start_model, v_basis, u_basis, records, tile_ranks, window_start, window_stop):
    tile_count = lax.axis_size("tile")
    device = lax.axis_index("tile")
    freq_count, rows_count, cols_count = tile_ranks.shape
    rank_total = v_basis.shape[1]
    pieces = tile_count // rows_count
    my_freq = device // cols_count
    my_col = device % cols_count
    my_row = device // pieces
    down_offsets = starts_along(tile_ranks, 1)
    side_offsets = starts_along(tile_ranks, 2)
    column_ranks = lax.dynamic_index_in_dim(
        lax.dynamic_index_in_dim(tile_ranks, my_freq, 0, False), my_col, 1, False
    )
    column_starts = lax.dynamic_index_in_dim(
        lax.dynamic_index_in_dim(down_offsets, my_freq, 0, False), my_col, 1, False
    )
    row_ranks = lax.dynamic_index_in_dim(tile_ranks, my_row, 1, False)
    row_starts = lax.dynamic_index_in_dim(side_offsets, my_row, 1, False)
    fwd_rank = jnp.broadcast_to(column_ranks[:, None], (rows_count, pieces)).reshape(tile_count)
    fwd_start = jnp.broadcast_to(column_starts[:, None], (rows_count, pieces)).reshape(tile_count)
    dest_freq = jnp.arange(tile_count, dtype=jnp.int32) // cols_count
    adj_rank = row_ranks.reshape(tile_count)
    adj_start = row_starts.reshape(tile_count) + dest_freq * rank_total
    cos_table, sin_table = wave_tables(freq_count, records.shape[0])
    moments = jnp.arange(records.shape[0], dtype=jnp.int32)[:, None, None]
    inside = (moments >= window_start[None]) & (moments < window_stop[None])
    observed = records.astype(jnp.float32)
    current = start_model
    for iteration in range(ITERS):
        rounded = current.astype(jnp.bfloat16)
        coeff_real = jnp.dot(v_basis[0], rounded[0], preferred_element_type=jnp.float32) - jnp.dot(
            v_basis[1], rounded[1], preferred_element_type=jnp.float32
        )
        coeff_imag = jnp.dot(v_basis[0], rounded[1], preferred_element_type=jnp.float32) + jnp.dot(
            v_basis[1], rounded[0], preferred_element_type=jnp.float32
        )
        coefficients = jnp.stack([coeff_real, coeff_imag]).astype(jnp.bfloat16)
        outbound = pack_slots(coefficients, fwd_rank, fwd_start)
        forward_received = lax.all_to_all(outbound, "tile", split_axis=1, concat_axis=1, tiled=True)
        grouped_cols = forward_received.reshape(
            2, freq_count, cols_count, RMAX, forward_received.shape[3]
        )
        forward_chosen = jnp.stack(
            [join_slots(grouped_cols[:, f], row_starts[f], rank_total) for f in range(freq_count)],
            axis=1,
        )
        pred_real = jnp.einsum(
            "fks,fkn->fsn", forward_chosen[0], u_basis[0], preferred_element_type=jnp.float32
        ) - jnp.einsum(
            "fks,fkn->fsn", forward_chosen[1], u_basis[1], preferred_element_type=jnp.float32
        )
        pred_imag = jnp.einsum(
            "fks,fkn->fsn", forward_chosen[0], u_basis[1], preferred_element_type=jnp.float32
        ) + jnp.einsum(
            "fks,fkn->fsn", forward_chosen[1], u_basis[0], preferred_element_type=jnp.float32
        )
        predicted = jnp.stack([pred_real, pred_imag])
        traces = jnp.einsum("ft,fsn->tsn", cos_table, predicted[0], precision=precise) - jnp.einsum(
            "ft,fsn->tsn", sin_table, predicted[1], precision=precise
        )
        residual = jnp.where(inside, traces - observed, jnp.zeros((), jnp.float32))
        back_real = jnp.einsum("ft,tsn->fsn", cos_table, residual, precision=precise)
        back_imag = -jnp.einsum("ft,tsn->fsn", sin_table, residual, precision=precise)
        adjoint_field = jnp.stack([back_real, back_imag]).astype(jnp.bfloat16)
        part_real = jnp.einsum(
            "fkn,fsn->fks", u_basis[0], adjoint_field[0], preferred_element_type=jnp.float32
        ) + jnp.einsum(
            "fkn,fsn->fks", u_basis[1], adjoint_field[1], preferred_element_type=jnp.float32
        )
        part_imag = jnp.einsum(
            "fkn,fsn->fks", u_basis[0], adjoint_field[1], preferred_element_type=jnp.float32
        ) - jnp.einsum(
            "fkn,fsn->fks", u_basis[1], adjoint_field[0], preferred_element_type=jnp.float32
        )
        partial_value = jnp.stack([part_real, part_imag]).astype(jnp.bfloat16)
        flat_partial = partial_value.reshape(2, freq_count * rank_total, partial_value.shape[3])
        outgoing = pack_slots(flat_partial, adj_rank, adj_start)
        received = lax.all_to_all(outgoing, "tile", split_axis=1, concat_axis=1, tiled=True)
        grouped_rows = received.reshape(2, rows_count, pieces, RMAX, received.shape[3])
        adjoint_summed = piece_tree(grouped_rows, 2)
        chosen = join_slots(adjoint_summed, column_starts, rank_total)
        contract_dims = (((0,), (0,)), ((), ()))
        grad_real = lax.dot_general(
            v_basis[0], chosen[0], contract_dims, preferred_element_type=jnp.float32
        ) + lax.dot_general(
            v_basis[1], chosen[1], contract_dims, preferred_element_type=jnp.float32
        )
        grad_imag = lax.dot_general(
            v_basis[0], chosen[1], contract_dims, preferred_element_type=jnp.float32
        ) - lax.dot_general(
            v_basis[1], chosen[0], contract_dims, preferred_element_type=jnp.float32
        )
        gradient = jnp.stack([grad_real, grad_imag])
        current = current - step_size * gradient
    return current


LANES = 128
CHUNKS = 1
PARTS = 2
f32 = jnp.float32
bf16 = jnp.bfloat16
far = pl.BlockSpec(memory_space=pltpu.HBM)
near = pl.BlockSpec(memory_space=pltpu.VMEM)


def dot_last(a, b):
    return lax.dot_general(a, b, (((1,), (1,)), ((), ())), preferred_element_type=f32)


def dot_first(a, b):
    return lax.dot_general(a, b, (((0,), (0,)), ((), ())), preferred_element_type=f32)


def xor_peer(me, mask, n):
    peer = me
    bit = 1
    while bit < n:
        if mask & bit:
            peer = peer + bit * (1 - 2 * ((me // bit) % 2))
        bit *= 2
    return peer


def add_windows(record_ref, open_ref, close_ref, sums_ref, first, count):
    sample_count = record_ref.shape[0]
    scale = math.sqrt(2.0 / sample_count)
    step, strip = 16, 4 * LANES
    strips = record_ref.shape[2] // strip

    def block(k, carry):
        rows = pl.ds(pl.multiple_of(first + (k // strips) * step, step), step)
        lanes = pl.ds(pl.multiple_of((k % strips) * strip, strip), strip)
        opened = open_ref[rows, lanes]
        closed = close_ref[rows, lanes]
        sums = [jnp.zeros(opened.shape, f32)] * 5
        for t in range(sample_count - 1):
            phase = 2.0 * math.pi / sample_count * t
            c, s = math.cos(phase) * scale, math.sin(phase) * scale
            seen = record_ref[t, rows, lanes].astype(f32)
            squares = (c * c, c * s, s * s)
            if sample_count // 4 <= t < sample_count // 2:
                terms = list(squares)
            else:
                inside = (t >= opened) if t < sample_count // 4 else (t < closed)
                seen = jnp.where(inside, seen, 0.0)
                terms = [jnp.where(inside, w, 0.0) for w in squares]
            terms += [seen * c, seen * s]
            sums = [x + y for x, y in zip(sums, terms)]
        for m in range(5):
            sums_ref[m, rows, lanes] = sums[m]
        return carry

    lax.fori_loop(0, (count // step) * strips, block, 0)


def fused_kernel(
    n, rank_hbm, x_hbm, v_hbm, u_hbm, record_hbm, open_hbm, close_hbm, out_ref,
    rank_ref, x_ref, v_ref, u_ref, record_ref, open_ref, close_ref,
    xw_ref, xt_ref, sums_ref, rows_ref, slots_ref, joined_ref, send_ref, recv_ref,
    start_ref, table_ref, load_sem, v_sem, send_sem, recv_sem,
):
    me = lax.axis_index("tile")
    masks = list(range(n - 1, 0, -1))
    peers = [xor_peer(me, mask, n) for mask in masks]
    _, total, width = v_ref.shape
    sources = x_ref.shape[2]
    half = sources // 2
    batches = 2
    blocks = total // 8

    loads = [
        pltpu.make_async_copy(source, target, load_sem.at[k])
        for k, (source, target) in enumerate(
            [
                (x_hbm, x_ref),
                (rank_hbm, rank_ref),
                (open_hbm, open_ref),
                (close_hbm, close_ref),
                (record_hbm, record_ref),
                (u_hbm, u_ref),
            ]
        )
    ]
    part = total // CHUNKS
    v_loads = [
        pltpu.make_async_copy(
            v_hbm.at[:, pl.ds(k * part, part)], v_ref.at[:, pl.ds(k * part, part)], v_sem.at[k]
        )
        for k in range(CHUNKS)
    ]
    loads[0].start()
    for load in v_loads:
        load.start()
    loads[1].start()

    barrier = pltpu.get_barrier_semaphore()
    for peer in peers:
        pl.semaphore_signal(
            barrier, inc=1, device_id={"tile": peer}, device_id_type=pl.DeviceIdType.MESH
        )

    for b in range(batches):
        rows_ref[b, pl.ds(total, RMAX), :] = jnp.zeros((RMAX, LANES), f32)

    def copy_of(e, b, d):
        return pltpu.make_async_remote_copy(
            src_ref=send_ref.at[e, b, d],
            dst_ref=recv_ref.at[e, b, me],
            send_sem=send_sem.at[e, b, d],
            recv_sem=recv_sem.at[e, b, d],
            device_id={"tile": peers[d]},
            device_id_type=pl.DeviceIdType.MESH,
        )

    def send_rows(e, b, side):
        def slot(k):
            return rows_ref[b, pl.ds(start_ref[side, k], RMAX), :].astype(bf16)

        for d, peer in enumerate(peers):
            send_ref[e, b, d] = slot(peer)
            copy_of(e, b, d).start()
        recv_ref[e, b, me] = slot(me)

    def join(e, b, side):
        for d in range(n - 1):
            copy_of(e, b, d).wait_recv()
        for k in range(n):
            slots_ref[pl.ds(k * RMAX, RMAX), :] = recv_ref[e, b, k].astype(f32)
        row = lax.broadcasted_iota(jnp.int32, (8, LANES), 0)

        def group(k):
            first = slots_ref[pl.ds(table_ref[side, 0, k], 8), :]
            second = slots_ref[pl.ds(table_ref[side, 1, k], 8), :]
            return jnp.where(row < table_ref[side, 2, k], first, second)

        for k in range(0, blocks, 2):
            pair = jnp.concatenate([group(k), group(k + 1)], axis=0)
            joined_ref[pl.ds(k * 8, 16), :] = pair.astype(bf16)

    lane = lax.broadcasted_iota(jnp.int32, (width, sources), 1)
    loads[0].wait()
    xr, xi = x_ref[0], x_ref[1]
    turned_r, turned_i = pltpu.roll(xr, half, 1), pltpu.roll(xi, half, 1)
    low = lane < half
    xw_ref[0, :, :sources] = jnp.where(low, xr, turned_i).astype(bf16)
    xw_ref[0, :, sources:] = jnp.where(low, turned_r, xi).astype(bf16)
    xw_ref[1, :, :sources] = jnp.where(low, -xi, turned_r).astype(bf16)
    xw_ref[1, :, sources:] = jnp.where(low, -turned_i, xr).astype(bf16)
    for k in range(CHUNKS):
        v_loads[k].wait()
        if k + 1 == CHUNKS:
            for load in loads[2:]:
                load.start()
        rows = pl.ds(k * part, part)
        value = jnp.dot(v_ref[0, rows, :], xw_ref[0], preferred_element_type=f32) + jnp.dot(
            v_ref[1, rows, :], xw_ref[1], preferred_element_type=f32
        )
        rows_ref[0, rows, :] = value[:, :LANES]
        rows_ref[1, rows, :] = value[:, LANES:]
    loads[1].wait()
    row_start, column_start = 0, 0
    for k in range(n):
        start_ref[0, k] = row_start
        start_ref[1, k] = column_start
        row_start = row_start + rank_ref[me, k]
        column_start = column_start + rank_ref[k, me]
    pl.semaphore_wait(barrier, n - 1)
    for b in range(batches):
        send_rows(0, b, 1)

    for side in range(2):

        def entry(k, carry):
            tile, start = carry
            end = start + (rank_ref[me, tile] if side == 0 else rank_ref[tile, me])
            table_ref[side, 0, k] = jnp.clip(tile * RMAX + k * 8 - start, 0, n * RMAX)
            table_ref[side, 1, k] = jnp.clip((tile + 1) * RMAX + k * 8 - end, 0, n * RMAX)
            table_ref[side, 2, k] = end - k * 8
            leave = end <= k * 8 + 8
            later = jnp.minimum(tile + 1, n - 1)
            return jnp.where(leave, later, tile), jnp.where(leave, end, start)

        lax.fori_loop(0, blocks, entry, (jnp.int32(0), jnp.int32(0)))
    slots_ref[pl.ds(n * RMAX, 8), :] = jnp.zeros((8, LANES), f32)
    for p in range(2):
        turned = x_ref[p].T
        for b in range(batches):
            xt_ref[b, pl.ds(p * half, half), :] = turned[b * half : (b + 1) * half]
    for load in loads[2:]:
        load.wait()

    def field_of(b):
        c = joined_ref[...]
        p = dot_first(c, u_ref[0])
        q = dot_first(c, u_ref[1])
        yr = p[:half] - q[half:]
        yi = q[:half] + p[half:]
        rows = pl.ds(pl.multiple_of(b * half, half), half)
        hr = sums_ref[0, rows, :] * yr - sums_ref[1, rows, :] * yi - sums_ref[3, rows, :]
        hi = sums_ref[2, rows, :] * yi - sums_ref[1, rows, :] * yr + sums_ref[4, rows, :]
        return hr.astype(bf16), hi.astype(bf16)

    def step_model(b):
        a = joined_ref[...]
        p = dot_first(a, v_ref[0])
        q = dot_first(a, v_ref[1])
        xr = xt_ref[b, :half, :] - step_size * (p[:half] + q[half:])
        xi = xt_ref[b, half:, :] - step_size * (p[half:] - q[:half])
        return xr, xi

    for iteration in range(ITERS):
        e = 2 * iteration

        def residual_step(b, carry):
            if iteration == 0:
                first = b * half
                add_windows(record_ref, open_ref, close_ref, sums_ref, first, half)
            join(e, b, 0)
            hr, hi = field_of(b)
            rows_ref[b, pl.ds(0, total), :] = dot_last(
                u_ref[0], jnp.concatenate([hr, hi], axis=0)
            ) + dot_last(u_ref[1], jnp.concatenate([hi, -hr], axis=0))
            send_rows(e + 1, b, 0)
            return carry

        lax.fori_loop(0, batches, residual_step, 0)
        if iteration + 1 < ITERS:

            def model_step(b, carry):
                join(e + 1, b, 1)
                xr, xi = step_model(b)
                xt_ref[b, :half, :] = xr
                xt_ref[b, half:, :] = xi
                xr, xi = xr.astype(bf16), xi.astype(bf16)
                rows_ref[b, pl.ds(0, total), :] = dot_last(
                    v_ref[0], jnp.concatenate([xr, xi], axis=0)
                ) + dot_last(v_ref[1], jnp.concatenate([-xi, xr], axis=0))
                send_rows(e + 2, b, 1)
                return carry

            lax.fori_loop(0, batches, model_step, 0)
        else:
            for b in range(batches):
                join(e + 1, b, 1)
                xr, xi = step_model(b)
                out_ref[b, :half, :] = xr
                out_ref[b, half:, :] = xi

    def finish(e, carry):
        for b in range(batches):
            for d in range(n - 1):
                copy_of(e, b, d).wait_send()
        return carry

    lax.fori_loop(0, 2 * ITERS, finish, 0)


def fused(start_model, v_basis, u_parts, records, ranks, window_start, window_stop):
    inputs = (ranks, start_model, v_basis, u_parts, records, window_start, window_stop)
    n = ranks.shape[0]
    _, width, sources = start_model.shape
    _, total, _ = v_basis.shape
    receivers = records.shape[2]
    exchanges, batches = 2 * ITERS, 2
    like = lambda a: pltpu.VMEM(a.shape, a.dtype)
    return pl.pallas_call(
        functools.partial(fused_kernel, n),
        out_shape=jax.ShapeDtypeStruct((batches, sources, width), f32),
        in_specs=[far] * 7,
        out_specs=near,
        scratch_shapes=[
            pltpu.SMEM(ranks.shape, ranks.dtype),
            like(start_model),
            like(v_basis),
            like(u_parts),
            like(records),
            like(window_start),
            like(window_stop),
            pltpu.VMEM((2, width, 2 * sources), bf16),
            pltpu.VMEM((batches, sources, width), f32),
            pltpu.VMEM((5, sources, receivers), f32),
            pltpu.VMEM((batches, total + RMAX, LANES), f32),
            pltpu.VMEM((n * RMAX + 8, LANES), f32),
            pltpu.VMEM((total, LANES), bf16),
            pltpu.VMEM((exchanges, batches, n - 1, RMAX, LANES), bf16),
            pltpu.VMEM((exchanges, batches, n, RMAX, LANES), bf16),
            pltpu.SMEM((2, n), jnp.int32),
            pltpu.SMEM((2, 3, total // 8), jnp.int32),
            pltpu.SemaphoreType.DMA((6,)),
            pltpu.SemaphoreType.DMA((CHUNKS,)),
            pltpu.SemaphoreType.DMA((exchanges, batches, n - 1)),
            pltpu.SemaphoreType.DMA((exchanges, batches, n - 1)),
        ],
        compiler_params=pltpu.CompilerParams(
            collective_id=0, has_side_effects=True, vmem_limit_bytes=44 * 1024 * 1024
        ),
    )(*[pltpu.with_memory_space_constraint(a, pltpu.HBM) for a in inputs])


def turn_kernel(xt_ref, out_ref):
    batches, sources, _ = xt_ref.shape
    half = sources // batches
    _, rows, _ = out_ref.shape
    lanes = pl.ds(pl.multiple_of(pl.program_id(0) * rows, rows), rows)
    for p in range(2):
        part = [xt_ref[b, p * half : (p + 1) * half, lanes] for b in range(batches)]
        out_ref[p] = jnp.concatenate(part, axis=0).T


def by_row(xt):
    _, sources, width = xt.shape
    rows = width // PARTS
    return pl.pallas_call(
        turn_kernel,
        grid=(PARTS,),
        out_shape=jax.ShapeDtypeStruct((2, width, sources), xt.dtype),
        in_specs=[near],
        out_specs=pl.BlockSpec((2, rows, sources), lambda k: (0, k, 0)),
        compiler_params=pltpu.CompilerParams(vmem_limit_bytes=16 * 1024 * 1024),
    )(xt)


def on_device(start_model, v_basis, u_basis, records, tile_ranks, window_start, window_stop):
    n = lax.axis_size("tile")
    freq_count, rows_count, cols_count = tile_ranks.shape
    single = freq_count == 1 and n == rows_count and n == cols_count and n & (n - 1) == 0
    fits = start_model.shape[2] == LANES and v_basis.shape[1] % (16 * CHUNKS) == 0
    fits = fits and records.shape[2] % (4 * LANES) == 0 and start_model.shape[1] % LANES == 0
    if not (single and fits):
        return on_device_general(
            start_model, v_basis, u_basis, records, tile_ranks, window_start, window_stop
        )
    xt = fused(
        start_model, v_basis, u_basis[:, 0], records, tile_ranks[0], window_start, window_stop
    )
    return by_row(xt)


def solution(mesh):
    in_specs = (
        P(None, ("groups", "tile"), None),
        P(None, ("groups", "tile"), None),
        P(None, None, None, ("groups", "tile")),
        P(None, None, ("groups", "tile")),
        P("groups", None, None),
        P(None, ("groups", "tile")),
        P(None, ("groups", "tile")),
    )
    out_specs = P(None, ("groups", "tile"), None)
    return jax.shard_map(
        on_device, mesh=mesh, in_specs=in_specs, out_specs=out_specs, check_vma=False
    )
```

```python
import functools
import math

import jax
import jax.numpy as jnp
from jax import lax
from jax.experimental import pallas as pl
from jax.experimental.pallas import tpu as pltpu
from jax.sharding import PartitionSpec as P

RMAX = 96
ITERS = 2


step_size = 0.5
precise = lax.Precision.HIGHEST


def wave_tables(bin_count, sample_count):
    moments = jnp.arange(sample_count, dtype=jnp.float32)
    bin_ids = jnp.arange(bin_count, dtype=jnp.float32) + 1.0
    phases = 2.0 * math.pi / sample_count * bin_ids[:, None] * moments[None, :]
    factor = math.sqrt(2.0 / sample_count)
    return (jnp.cos(phases) * factor, jnp.sin(phases) * factor)


def piece_tree(partials, axis):
    current = partials
    while current.shape[axis] > 1:
        half_count = current.shape[axis] // 2
        lower_part = lax.slice_in_dim(current, 0, half_count, axis=axis).astype(jnp.float32)
        upper_part = lax.slice_in_dim(current, half_count, 2 * half_count, axis=axis).astype(
            jnp.float32
        )
        current = (lower_part + upper_part).astype(jnp.bfloat16)
    return jnp.squeeze(current, axis)


def starts_along(tile_ranks, axis):
    count = tile_ranks.shape[axis]
    return jnp.concatenate(
        [
            jnp.sum(lax.slice_in_dim(tile_ranks, 0, k, axis=axis), axis=axis, keepdims=True)
            for k in range(count)
        ],
        axis=axis,
    ).astype(jnp.int32)


def pack_slots(source_rows, rank_each, start_each):
    padded = jnp.pad(source_rows, ((0, 0), (0, RMAX), (0, 0)))
    live = jnp.arange(RMAX, dtype=jnp.int32)[None, :, None]

    def cut(operands):
        rank, start = operands
        rows = lax.dynamic_slice_in_dim(padded, start, RMAX, axis=1)
        return jnp.where(live < rank, rows, jnp.zeros((), rows.dtype))

    return jnp.moveaxis(lax.map(cut, (rank_each, start_each)), 0, 1)


def join_slots(slots, starts, total):
    joined = jnp.zeros((slots.shape[0], total + RMAX, slots.shape[3]), slots.dtype)

    def place(k, joined):
        rows = lax.dynamic_index_in_dim(slots, k, 1, False)
        return lax.dynamic_update_slice_in_dim(joined, rows, starts[k], axis=1)

    return lax.fori_loop(0, slots.shape[1], place, joined)[:, :total]


def on_device_general(start_model, v_basis, u_basis, records, tile_ranks, window_start, window_stop):
    tile_count = lax.axis_size("tile")
    device = lax.axis_index("tile")
    freq_count, rows_count, cols_count = tile_ranks.shape
    rank_total = v_basis.shape[1]
    pieces = tile_count // rows_count
    my_freq = device // cols_count
    my_col = device % cols_count
    my_row = device // pieces
    down_offsets = starts_along(tile_ranks, 1)
    side_offsets = starts_along(tile_ranks, 2)
    column_ranks = lax.dynamic_index_in_dim(
        lax.dynamic_index_in_dim(tile_ranks, my_freq, 0, False), my_col, 1, False
    )
    column_starts = lax.dynamic_index_in_dim(
        lax.dynamic_index_in_dim(down_offsets, my_freq, 0, False), my_col, 1, False
    )
    row_ranks = lax.dynamic_index_in_dim(tile_ranks, my_row, 1, False)
    row_starts = lax.dynamic_index_in_dim(side_offsets, my_row, 1, False)
    fwd_rank = jnp.broadcast_to(column_ranks[:, None], (rows_count, pieces)).reshape(tile_count)
    fwd_start = jnp.broadcast_to(column_starts[:, None], (rows_count, pieces)).reshape(tile_count)
    dest_freq = jnp.arange(tile_count, dtype=jnp.int32) // cols_count
    adj_rank = row_ranks.reshape(tile_count)
    adj_start = row_starts.reshape(tile_count) + dest_freq * rank_total
    cos_table, sin_table = wave_tables(freq_count, records.shape[0])
    moments = jnp.arange(records.shape[0], dtype=jnp.int32)[:, None, None]
    inside = (moments >= window_start[None]) & (moments < window_stop[None])
    observed = records.astype(jnp.float32)
    current = start_model
    for iteration in range(ITERS):
        rounded = current.astype(jnp.bfloat16)
        coeff_real = jnp.dot(v_basis[0], rounded[0], preferred_element_type=jnp.float32) - jnp.dot(
            v_basis[1], rounded[1], preferred_element_type=jnp.float32
        )
        coeff_imag = jnp.dot(v_basis[0], rounded[1], preferred_element_type=jnp.float32) + jnp.dot(
            v_basis[1], rounded[0], preferred_element_type=jnp.float32
        )
        coefficients = jnp.stack([coeff_real, coeff_imag]).astype(jnp.bfloat16)
        outbound = pack_slots(coefficients, fwd_rank, fwd_start)
        forward_received = lax.all_to_all(outbound, "tile", split_axis=1, concat_axis=1, tiled=True)
        grouped_cols = forward_received.reshape(
            2, freq_count, cols_count, RMAX, forward_received.shape[3]
        )
        forward_chosen = jnp.stack(
            [join_slots(grouped_cols[:, f], row_starts[f], rank_total) for f in range(freq_count)],
            axis=1,
        )
        pred_real = jnp.einsum(
            "fks,fkn->fsn", forward_chosen[0], u_basis[0], preferred_element_type=jnp.float32
        ) - jnp.einsum(
            "fks,fkn->fsn", forward_chosen[1], u_basis[1], preferred_element_type=jnp.float32
        )
        pred_imag = jnp.einsum(
            "fks,fkn->fsn", forward_chosen[0], u_basis[1], preferred_element_type=jnp.float32
        ) + jnp.einsum(
            "fks,fkn->fsn", forward_chosen[1], u_basis[0], preferred_element_type=jnp.float32
        )
        predicted = jnp.stack([pred_real, pred_imag])
        traces = jnp.einsum("ft,fsn->tsn", cos_table, predicted[0], precision=precise) - jnp.einsum(
            "ft,fsn->tsn", sin_table, predicted[1], precision=precise
        )
        residual = jnp.where(inside, traces - observed, jnp.zeros((), jnp.float32))
        back_real = jnp.einsum("ft,tsn->fsn", cos_table, residual, precision=precise)
        back_imag = -jnp.einsum("ft,tsn->fsn", sin_table, residual, precision=precise)
        adjoint_field = jnp.stack([back_real, back_imag]).astype(jnp.bfloat16)
        part_real = jnp.einsum(
            "fkn,fsn->fks", u_basis[0], adjoint_field[0], preferred_element_type=jnp.float32
        ) + jnp.einsum(
            "fkn,fsn->fks", u_basis[1], adjoint_field[1], preferred_element_type=jnp.float32
        )
        part_imag = jnp.einsum(
            "fkn,fsn->fks", u_basis[0], adjoint_field[1], preferred_element_type=jnp.float32
        ) - jnp.einsum(
            "fkn,fsn->fks", u_basis[1], adjoint_field[0], preferred_element_type=jnp.float32
        )
        partial_value = jnp.stack([part_real, part_imag]).astype(jnp.bfloat16)
        flat_partial = partial_value.reshape(2, freq_count * rank_total, partial_value.shape[3])
        outgoing = pack_slots(flat_partial, adj_rank, adj_start)
        received = lax.all_to_all(outgoing, "tile", split_axis=1, concat_axis=1, tiled=True)
        grouped_rows = received.reshape(2, rows_count, pieces, RMAX, received.shape[3])
        adjoint_summed = piece_tree(grouped_rows, 2)
        chosen = join_slots(adjoint_summed, column_starts, rank_total)
        contract_dims = (((0,), (0,)), ((), ()))
        grad_real = lax.dot_general(
            v_basis[0], chosen[0], contract_dims, preferred_element_type=jnp.float32
        ) + lax.dot_general(
            v_basis[1], chosen[1], contract_dims, preferred_element_type=jnp.float32
        )
        grad_imag = lax.dot_general(
            v_basis[0], chosen[1], contract_dims, preferred_element_type=jnp.float32
        ) - lax.dot_general(
            v_basis[1], chosen[0], contract_dims, preferred_element_type=jnp.float32
        )
        gradient = jnp.stack([grad_real, grad_imag])
        current = current - step_size * gradient
    return current


LANES = 128
CHUNKS = 1
PARTS = 2
f32 = jnp.float32
bf16 = jnp.bfloat16
far = pl.BlockSpec(memory_space=pltpu.HBM)
near = pl.BlockSpec(memory_space=pltpu.VMEM)


def dot_last(a, b):
    return lax.dot_general(a, b, (((1,), (1,)), ((), ())), preferred_element_type=f32)


def dot_first(a, b):
    return lax.dot_general(a, b, (((0,), (0,)), ((), ())), preferred_element_type=f32)


def xor_peer(me, mask, n):
    peer = me
    bit = 1
    while bit < n:
        if mask & bit:
            peer = peer + bit * (1 - 2 * ((me // bit) % 2))
        bit *= 2
    return peer


def add_windows(record_ref, open_ref, close_ref, sums_ref, first, count):
    sample_count = record_ref.shape[0]
    scale = math.sqrt(2.0 / sample_count)
    step, strip = 16, 4 * LANES
    strips = record_ref.shape[2] // strip

    def block(k, carry):
        rows = pl.ds(pl.multiple_of(first + (k // strips) * step, step), step)
        lanes = pl.ds(pl.multiple_of((k % strips) * strip, strip), strip)
        opened = open_ref[rows, lanes]
        closed = close_ref[rows, lanes]
        sums = [jnp.zeros(opened.shape, f32)] * 5
        for t in range(sample_count - 1):
            phase = 2.0 * math.pi / sample_count * t
            c, s = math.cos(phase) * scale, math.sin(phase) * scale
            seen = record_ref[t, rows, lanes].astype(f32)
            squares = (c * c, c * s, s * s)
            if sample_count // 4 <= t < sample_count // 2:
                terms = list(squares)
            else:
                inside = (t >= opened) if t < sample_count // 4 else (t < closed)
                seen = jnp.where(inside, seen, 0.0)
                terms = [jnp.where(inside, w, 0.0) for w in squares]
            terms += [seen * c, seen * s]
            sums = [x + y for x, y in zip(sums, terms)]
        for m in range(5):
            sums_ref[m, rows, lanes] = sums[m]
        return carry

    lax.fori_loop(0, (count // step) * strips, block, 0)


def fused_kernel(
    n, rank_hbm, x_hbm, v_hbm, u_hbm, record_hbm, open_hbm, close_hbm, out_ref,
    rank_ref, x_ref, v_ref, u_ref, record_ref, open_ref, close_ref,
    xw_ref, xt_ref, sums_ref, rows_ref, slots_ref, joined_ref, send_ref, recv_ref,
    start_ref, table_ref, load_sem, v_sem, send_sem, recv_sem,
):
    me = lax.axis_index("tile")
    masks = list(range(n - 1, 0, -1))
    peers = [xor_peer(me, mask, n) for mask in masks]
    _, total, width = v_ref.shape
    sources = x_ref.shape[2]
    half = sources // 2
    batches = 2
    blocks = total // 8

    loads = [
        pltpu.make_async_copy(source, target, load_sem.at[k])
        for k, (source, target) in enumerate(
            [
                (x_hbm, x_ref),
                (rank_hbm, rank_ref),
                (open_hbm, open_ref),
                (close_hbm, close_ref),
                (record_hbm, record_ref),
                (u_hbm, u_ref),
            ]
        )
    ]
    part = total // CHUNKS
    v_loads = [
        pltpu.make_async_copy(
            v_hbm.at[:, pl.ds(k * part, part)], v_ref.at[:, pl.ds(k * part, part)], v_sem.at[k]
        )
        for k in range(CHUNKS)
    ]
    loads[0].start()
    for load in v_loads:
        load.start()
    loads[1].start()

    barrier = pltpu.get_barrier_semaphore()
    for peer in peers:
        pl.semaphore_signal(
            barrier, inc=1, device_id={"tile": peer}, device_id_type=pl.DeviceIdType.MESH
        )

    for b in range(batches):
        rows_ref[b, pl.ds(total, RMAX), :] = jnp.zeros((RMAX, LANES), f32)

    def copy_of(e, b, d):
        return pltpu.make_async_remote_copy(
            src_ref=send_ref.at[e, b, d],
            dst_ref=recv_ref.at[e, b, me],
            send_sem=send_sem.at[e, b],
            recv_sem=recv_sem.at[e, b],
            device_id={"tile": peers[d]},
            device_id_type=pl.DeviceIdType.MESH,
        )

    def all_of(e, b):
        return pltpu.make_async_remote_copy(
            src_ref=send_ref.at[e, b],
            dst_ref=recv_ref.at[e, b, pl.ds(0, n - 1)],
            send_sem=send_sem.at[e, b],
            recv_sem=recv_sem.at[e, b],
            device_id={"tile": peers[0]},
            device_id_type=pl.DeviceIdType.MESH,
        )

    def send_rows(e, b, side):
        def slot(k):
            return rows_ref[b, pl.ds(start_ref[side, k], RMAX), :].astype(bf16)

        for d, peer in enumerate(peers):
            send_ref[e, b, d] = slot(peer)
            copy_of(e, b, d).start()
        recv_ref[e, b, me] = slot(me)

    def join(e, b, side):
        all_of(e, b).wait_recv()
        for k in range(n):
            slots_ref[pl.ds(k * RMAX, RMAX), :] = recv_ref[e, b, k].astype(f32)
        row = lax.broadcasted_iota(jnp.int32, (8, LANES), 0)

        def group(k):
            first = slots_ref[pl.ds(table_ref[side, 0, k], 8), :]
            second = slots_ref[pl.ds(table_ref[side, 1, k], 8), :]
            return jnp.where(row < table_ref[side, 2, k], first, second)

        for k in range(0, blocks, 2):
            pair = jnp.concatenate([group(k), group(k + 1)], axis=0)
            joined_ref[pl.ds(k * 8, 16), :] = pair.astype(bf16)

    lane = lax.broadcasted_iota(jnp.int32, (width, sources), 1)
    loads[0].wait()
    xr, xi = x_ref[0], x_ref[1]
    turned_r, turned_i = pltpu.roll(xr, half, 1), pltpu.roll(xi, half, 1)
    low = lane < half
    xw_ref[0, :, :sources] = jnp.where(low, xr, turned_i).astype(bf16)
    xw_ref[0, :, sources:] = jnp.where(low, turned_r, xi).astype(bf16)
    xw_ref[1, :, :sources] = jnp.where(low, -xi, turned_r).astype(bf16)
    xw_ref[1, :, sources:] = jnp.where(low, -turned_i, xr).astype(bf16)
    for k in range(CHUNKS):
        v_loads[k].wait()
        if k + 1 == CHUNKS:
            for load in loads[2:]:
                load.start()
        rows = pl.ds(k * part, part)
        value = jnp.dot(v_ref[0, rows, :], xw_ref[0], preferred_element_type=f32) + jnp.dot(
            v_ref[1, rows, :], xw_ref[1], preferred_element_type=f32
        )
        rows_ref[0, rows, :] = value[:, :LANES]
        rows_ref[1, rows, :] = value[:, LANES:]
    loads[1].wait()
    row_start, column_start = 0, 0
    for k in range(n):
        start_ref[0, k] = row_start
        start_ref[1, k] = column_start
        row_start = row_start + rank_ref[me, k]
        column_start = column_start + rank_ref[k, me]
    pl.semaphore_wait(barrier, n - 1)
    for b in range(batches):
        send_rows(0, b, 1)

    for side in range(2):

        def entry(k, carry):
            tile, start = carry
            end = start + (rank_ref[me, tile] if side == 0 else rank_ref[tile, me])
            table_ref[side, 0, k] = jnp.clip(tile * RMAX + k * 8 - start, 0, n * RMAX)
            table_ref[side, 1, k] = jnp.clip((tile + 1) * RMAX + k * 8 - end, 0, n * RMAX)
            table_ref[side, 2, k] = end - k * 8
            leave = end <= k * 8 + 8
            later = jnp.minimum(tile + 1, n - 1)
            return jnp.where(leave, later, tile), jnp.where(leave, end, start)

        lax.fori_loop(0, blocks, entry, (jnp.int32(0), jnp.int32(0)))
    slots_ref[pl.ds(n * RMAX, 8), :] = jnp.zeros((8, LANES), f32)
    for p in range(2):
        turned = x_ref[p].T
        for b in range(batches):
            xt_ref[b, pl.ds(p * half, half), :] = turned[b * half : (b + 1) * half]
    for load in loads[2:]:
        load.wait()

    def field_of(b):
        c = joined_ref[...]
        p = dot_first(c, u_ref[0])
        q = dot_first(c, u_ref[1])
        yr = p[:half] - q[half:]
        yi = q[:half] + p[half:]
        rows = pl.ds(pl.multiple_of(b * half, half), half)
        hr = sums_ref[0, rows, :] * yr - sums_ref[1, rows, :] * yi - sums_ref[3, rows, :]
        hi = sums_ref[2, rows, :] * yi - sums_ref[1, rows, :] * yr + sums_ref[4, rows, :]
        return hr.astype(bf16), hi.astype(bf16)

    def step_model(b):
        a = joined_ref[...]
        p = dot_first(a, v_ref[0])
        q = dot_first(a, v_ref[1])
        xr = xt_ref[b, :half, :] - step_size * (p[:half] + q[half:])
        xi = xt_ref[b, half:, :] - step_size * (p[half:] - q[:half])
        return xr, xi

    for iteration in range(ITERS):
        e = 2 * iteration

        def residual_step(b, carry):
            if iteration == 0:
                first = b * half
                add_windows(record_ref, open_ref, close_ref, sums_ref, first, half)
            join(e, b, 0)
            hr, hi = field_of(b)
            rows_ref[b, pl.ds(0, total), :] = dot_last(
                u_ref[0], jnp.concatenate([hr, hi], axis=0)
            ) + dot_last(u_ref[1], jnp.concatenate([hi, -hr], axis=0))
            send_rows(e + 1, b, 0)
            return carry

        lax.fori_loop(0, batches, residual_step, 0)
        if iteration + 1 < ITERS:

            def model_step(b, carry):
                join(e + 1, b, 1)
                xr, xi = step_model(b)
                xt_ref[b, :half, :] = xr
                xt_ref[b, half:, :] = xi
                xr, xi = xr.astype(bf16), xi.astype(bf16)
                rows_ref[b, pl.ds(0, total), :] = dot_last(
                    v_ref[0], jnp.concatenate([xr, xi], axis=0)
                ) + dot_last(v_ref[1], jnp.concatenate([-xi, xr], axis=0))
                send_rows(e + 2, b, 1)
                return carry

            lax.fori_loop(0, batches, model_step, 0)
        else:
            for b in range(batches):
                join(e + 1, b, 1)
                xr, xi = step_model(b)
                out_ref[b, :half, :] = xr
                out_ref[b, half:, :] = xi

    def finish(e, carry):
        for b in range(batches):
            all_of(e, b).wait_send()
        return carry

    lax.fori_loop(0, 2 * ITERS, finish, 0)


def fused(start_model, v_basis, u_parts, records, ranks, window_start, window_stop):
    inputs = (ranks, start_model, v_basis, u_parts, records, window_start, window_stop)
    n = ranks.shape[0]
    _, width, sources = start_model.shape
    _, total, _ = v_basis.shape
    receivers = records.shape[2]
    exchanges, batches = 2 * ITERS, 2
    like = lambda a: pltpu.VMEM(a.shape, a.dtype)
    return pl.pallas_call(
        functools.partial(fused_kernel, n),
        out_shape=jax.ShapeDtypeStruct((batches, sources, width), f32),
        in_specs=[far] * 7,
        out_specs=near,
        scratch_shapes=[
            pltpu.SMEM(ranks.shape, ranks.dtype),
            like(start_model),
            like(v_basis),
            like(u_parts),
            like(records),
            like(window_start),
            like(window_stop),
            pltpu.VMEM((2, width, 2 * sources), bf16),
            pltpu.VMEM((batches, sources, width), f32),
            pltpu.VMEM((5, sources, receivers), f32),
            pltpu.VMEM((batches, total + RMAX, LANES), f32),
            pltpu.VMEM((n * RMAX + 8, LANES), f32),
            pltpu.VMEM((total, LANES), bf16),
            pltpu.VMEM((exchanges, batches, n - 1, RMAX, LANES), bf16),
            pltpu.VMEM((exchanges, batches, n, RMAX, LANES), bf16),
            pltpu.SMEM((2, n), jnp.int32),
            pltpu.SMEM((2, 3, total // 8), jnp.int32),
            pltpu.SemaphoreType.DMA((6,)),
            pltpu.SemaphoreType.DMA((CHUNKS,)),
            pltpu.SemaphoreType.DMA((exchanges, batches)),
            pltpu.SemaphoreType.DMA((exchanges, batches)),
        ],
        compiler_params=pltpu.CompilerParams(
            collective_id=0, has_side_effects=True, vmem_limit_bytes=44 * 1024 * 1024
        ),
    )(*[pltpu.with_memory_space_constraint(a, pltpu.HBM) for a in inputs])


def turn_kernel(xt_ref, out_ref):
    batches, sources, _ = xt_ref.shape
    half = sources // batches
    _, rows, _ = out_ref.shape
    lanes = pl.ds(pl.multiple_of(pl.program_id(0) * rows, rows), rows)
    for p in range(2):
        part = [xt_ref[b, p * half : (p + 1) * half, lanes] for b in range(batches)]
        out_ref[p] = jnp.concatenate(part, axis=0).T


def by_row(xt):
    _, sources, width = xt.shape
    rows = width // PARTS
    return pl.pallas_call(
        turn_kernel,
        grid=(PARTS,),
        out_shape=jax.ShapeDtypeStruct((2, width, sources), xt.dtype),
        in_specs=[near],
        out_specs=pl.BlockSpec((2, rows, sources), lambda k: (0, k, 0)),
        compiler_params=pltpu.CompilerParams(vmem_limit_bytes=16 * 1024 * 1024),
    )(xt)


def on_device(start_model, v_basis, u_basis, records, tile_ranks, window_start, window_stop):
    n = lax.axis_size("tile")
    freq_count, rows_count, cols_count = tile_ranks.shape
    single = freq_count == 1 and n == rows_count and n == cols_count and n & (n - 1) == 0
    fits = start_model.shape[2] == LANES and v_basis.shape[1] % (16 * CHUNKS) == 0
    fits = fits and records.shape[2] % (4 * LANES) == 0 and start_model.shape[1] % LANES == 0
    if not (single and fits):
        return on_device_general(
            start_model, v_basis, u_basis, records, tile_ranks, window_start, window_stop
        )
    xt = fused(
        start_model, v_basis, u_basis[:, 0], records, tile_ranks[0], window_start, window_stop
    )
    return by_row(xt)


def solution(mesh):
    in_specs = (
        P(None, ("groups", "tile"), None),
        P(None, ("groups", "tile"), None),
        P(None, None, None, ("groups", "tile")),
        P(None, None, ("groups", "tile")),
        P("groups", None, None),
        P(None, ("groups", "tile")),
        P(None, ("groups", "tile")),
    )
    out_specs = P(None, ("groups", "tile"), None)
    return jax.shard_map(
        on_device, mesh=mesh, in_specs=in_specs, out_specs=out_specs, check_vma=False
    )
```

```python
import functools
import math

import jax
import jax.numpy as jnp
from jax import lax
from jax.experimental import pallas as pl
from jax.experimental.pallas import tpu as pltpu
from jax.sharding import PartitionSpec as P

RMAX = 96
ITERS = 2


step_size = 0.5
precise = lax.Precision.HIGHEST


def wave_tables(bin_count, sample_count):
    moments = jnp.arange(sample_count, dtype=jnp.float32)
    bin_ids = jnp.arange(bin_count, dtype=jnp.float32) + 1.0
    phases = 2.0 * math.pi / sample_count * bin_ids[:, None] * moments[None, :]
    factor = math.sqrt(2.0 / sample_count)
    return (jnp.cos(phases) * factor, jnp.sin(phases) * factor)


def piece_tree(partials, axis):
    current = partials
    while current.shape[axis] > 1:
        half_count = current.shape[axis] // 2
        lower_part = lax.slice_in_dim(current, 0, half_count, axis=axis).astype(jnp.float32)
        upper_part = lax.slice_in_dim(current, half_count, 2 * half_count, axis=axis).astype(
            jnp.float32
        )
        current = (lower_part + upper_part).astype(jnp.bfloat16)
    return jnp.squeeze(current, axis)


def starts_along(tile_ranks, axis):
    count = tile_ranks.shape[axis]
    return jnp.concatenate(
        [
            jnp.sum(lax.slice_in_dim(tile_ranks, 0, k, axis=axis), axis=axis, keepdims=True)
            for k in range(count)
        ],
        axis=axis,
    ).astype(jnp.int32)


def pack_slots(source_rows, rank_each, start_each):
    padded = jnp.pad(source_rows, ((0, 0), (0, RMAX), (0, 0)))
    live = jnp.arange(RMAX, dtype=jnp.int32)[None, :, None]

    def cut(operands):
        rank, start = operands
        rows = lax.dynamic_slice_in_dim(padded, start, RMAX, axis=1)
        return jnp.where(live < rank, rows, jnp.zeros((), rows.dtype))

    return jnp.moveaxis(lax.map(cut, (rank_each, start_each)), 0, 1)


def join_slots(slots, starts, total):
    joined = jnp.zeros((slots.shape[0], total + RMAX, slots.shape[3]), slots.dtype)

    def place(k, joined):
        rows = lax.dynamic_index_in_dim(slots, k, 1, False)
        return lax.dynamic_update_slice_in_dim(joined, rows, starts[k], axis=1)

    return lax.fori_loop(0, slots.shape[1], place, joined)[:, :total]


def on_device_general(start_model, v_basis, u_basis, records, tile_ranks, window_start, window_stop):
    tile_count = lax.axis_size("tile")
    device = lax.axis_index("tile")
    freq_count, rows_count, cols_count = tile_ranks.shape
    rank_total = v_basis.shape[1]
    pieces = tile_count // rows_count
    my_freq = device // cols_count
    my_col = device % cols_count
    my_row = device // pieces
    down_offsets = starts_along(tile_ranks, 1)
    side_offsets = starts_along(tile_ranks, 2)
    column_ranks = lax.dynamic_index_in_dim(
        lax.dynamic_index_in_dim(tile_ranks, my_freq, 0, False), my_col, 1, False
    )
    column_starts = lax.dynamic_index_in_dim(
        lax.dynamic_index_in_dim(down_offsets, my_freq, 0, False), my_col, 1, False
    )
    row_ranks = lax.dynamic_index_in_dim(tile_ranks, my_row, 1, False)
    row_starts = lax.dynamic_index_in_dim(side_offsets, my_row, 1, False)
    fwd_rank = jnp.broadcast_to(column_ranks[:, None], (rows_count, pieces)).reshape(tile_count)
    fwd_start = jnp.broadcast_to(column_starts[:, None], (rows_count, pieces)).reshape(tile_count)
    dest_freq = jnp.arange(tile_count, dtype=jnp.int32) // cols_count
    adj_rank = row_ranks.reshape(tile_count)
    adj_start = row_starts.reshape(tile_count) + dest_freq * rank_total
    cos_table, sin_table = wave_tables(freq_count, records.shape[0])
    moments = jnp.arange(records.shape[0], dtype=jnp.int32)[:, None, None]
    inside = (moments >= window_start[None]) & (moments < window_stop[None])
    observed = records.astype(jnp.float32)
    current = start_model
    for iteration in range(ITERS):
        rounded = current.astype(jnp.bfloat16)
        coeff_real = jnp.dot(v_basis[0], rounded[0], preferred_element_type=jnp.float32) - jnp.dot(
            v_basis[1], rounded[1], preferred_element_type=jnp.float32
        )
        coeff_imag = jnp.dot(v_basis[0], rounded[1], preferred_element_type=jnp.float32) + jnp.dot(
            v_basis[1], rounded[0], preferred_element_type=jnp.float32
        )
        coefficients = jnp.stack([coeff_real, coeff_imag]).astype(jnp.bfloat16)
        outbound = pack_slots(coefficients, fwd_rank, fwd_start)
        forward_received = lax.all_to_all(outbound, "tile", split_axis=1, concat_axis=1, tiled=True)
        grouped_cols = forward_received.reshape(
            2, freq_count, cols_count, RMAX, forward_received.shape[3]
        )
        forward_chosen = jnp.stack(
            [join_slots(grouped_cols[:, f], row_starts[f], rank_total) for f in range(freq_count)],
            axis=1,
        )
        pred_real = jnp.einsum(
            "fks,fkn->fsn", forward_chosen[0], u_basis[0], preferred_element_type=jnp.float32
        ) - jnp.einsum(
            "fks,fkn->fsn", forward_chosen[1], u_basis[1], preferred_element_type=jnp.float32
        )
        pred_imag = jnp.einsum(
            "fks,fkn->fsn", forward_chosen[0], u_basis[1], preferred_element_type=jnp.float32
        ) + jnp.einsum(
            "fks,fkn->fsn", forward_chosen[1], u_basis[0], preferred_element_type=jnp.float32
        )
        predicted = jnp.stack([pred_real, pred_imag])
        traces = jnp.einsum("ft,fsn->tsn", cos_table, predicted[0], precision=precise) - jnp.einsum(
            "ft,fsn->tsn", sin_table, predicted[1], precision=precise
        )
        residual = jnp.where(inside, traces - observed, jnp.zeros((), jnp.float32))
        back_real = jnp.einsum("ft,tsn->fsn", cos_table, residual, precision=precise)
        back_imag = -jnp.einsum("ft,tsn->fsn", sin_table, residual, precision=precise)
        adjoint_field = jnp.stack([back_real, back_imag]).astype(jnp.bfloat16)
        part_real = jnp.einsum(
            "fkn,fsn->fks", u_basis[0], adjoint_field[0], preferred_element_type=jnp.float32
        ) + jnp.einsum(
            "fkn,fsn->fks", u_basis[1], adjoint_field[1], preferred_element_type=jnp.float32
        )
        part_imag = jnp.einsum(
            "fkn,fsn->fks", u_basis[0], adjoint_field[1], preferred_element_type=jnp.float32
        ) - jnp.einsum(
            "fkn,fsn->fks", u_basis[1], adjoint_field[0], preferred_element_type=jnp.float32
        )
        partial_value = jnp.stack([part_real, part_imag]).astype(jnp.bfloat16)
        flat_partial = partial_value.reshape(2, freq_count * rank_total, partial_value.shape[3])
        outgoing = pack_slots(flat_partial, adj_rank, adj_start)
        received = lax.all_to_all(outgoing, "tile", split_axis=1, concat_axis=1, tiled=True)
        grouped_rows = received.reshape(2, rows_count, pieces, RMAX, received.shape[3])
        adjoint_summed = piece_tree(grouped_rows, 2)
        chosen = join_slots(adjoint_summed, column_starts, rank_total)
        contract_dims = (((0,), (0,)), ((), ()))
        grad_real = lax.dot_general(
            v_basis[0], chosen[0], contract_dims, preferred_element_type=jnp.float32
        ) + lax.dot_general(
            v_basis[1], chosen[1], contract_dims, preferred_element_type=jnp.float32
        )
        grad_imag = lax.dot_general(
            v_basis[0], chosen[1], contract_dims, preferred_element_type=jnp.float32
        ) - lax.dot_general(
            v_basis[1], chosen[0], contract_dims, preferred_element_type=jnp.float32
        )
        gradient = jnp.stack([grad_real, grad_imag])
        current = current - step_size * gradient
    return current


LANES = 128
PARTS = 2
f32 = jnp.float32
bf16 = jnp.bfloat16
far = pl.BlockSpec(memory_space=pltpu.HBM)
near = pl.BlockSpec(memory_space=pltpu.VMEM)


def dot_last(a, b):
    return lax.dot_general(a, b, (((1,), (1,)), ((), ())), preferred_element_type=f32)


def dot_first(a, b):
    return lax.dot_general(a, b, (((0,), (0,)), ((), ())), preferred_element_type=f32)


def xor_peer(me, mask, n):
    peer = me
    bit = 1
    while bit < n:
        if mask & bit:
            peer = peer + bit * (1 - 2 * ((me // bit) % 2))
        bit *= 2
    return peer


def add_windows(record_ref, open_ref, close_ref, sums_ref, first, count):
    sample_count = record_ref.shape[0]
    scale = math.sqrt(2.0 / sample_count)
    step, strip = 16, 4 * LANES
    strips = record_ref.shape[2] // strip

    def block(k, carry):
        rows = pl.ds(pl.multiple_of(first + (k // strips) * step, step), step)
        lanes = pl.ds(pl.multiple_of((k % strips) * strip, strip), strip)
        opened = open_ref[rows, lanes]
        closed = close_ref[rows, lanes]
        sums = [jnp.zeros(opened.shape, f32)] * 5
        for t in range(sample_count - 1):
            phase = 2.0 * math.pi / sample_count * t
            c, s = math.cos(phase) * scale, math.sin(phase) * scale
            seen = record_ref[t, rows, lanes].astype(f32)
            squares = (c * c, c * s, s * s)
            if sample_count // 4 <= t < sample_count // 2:
                terms = list(squares)
            else:
                inside = (t >= opened) if t < sample_count // 4 else (t < closed)
                seen = jnp.where(inside, seen, 0.0)
                terms = [jnp.where(inside, w, 0.0) for w in squares]
            terms += [seen * c, seen * s]
            sums = [x + y for x, y in zip(sums, terms)]
        for m in range(5):
            sums_ref[m, rows, lanes] = sums[m]
        return carry

    lax.fori_loop(0, (count // step) * strips, block, 0)


def fused_kernel(
    n, rank_hbm, x_hbm, v_hbm, u_hbm, record_hbm, open_hbm, close_hbm, out_ref,
    rank_ref, x_ref, v_ref, u_ref, record_ref, open_ref, close_ref,
    xw_ref, xt_ref, sums_ref, rows_ref, slots_ref, joined_ref, send_ref, recv_ref,
    start_ref, table_ref, load_sem, v_sem, send_sem, recv_sem,
):
    me = lax.axis_index("tile")
    masks = list(range(n // 2, n)) + list(range(n // 2 - 1, 0, -1))
    peers = [xor_peer(me, mask, n) for mask in masks]
    _, total, width = v_ref.shape
    sources = x_ref.shape[2]
    half = sources // 2
    batches = 2
    blocks = total // 8

    loads = [
        pltpu.make_async_copy(source, target, load_sem.at[k])
        for k, (source, target) in enumerate(
            [
                (x_hbm, x_ref),
                (rank_hbm, rank_ref),
                (open_hbm, open_ref),
                (close_hbm, close_ref),
                (record_hbm, record_ref),
                (u_hbm, u_ref),
            ]
        )
    ]
    v_loads = [pltpu.make_async_copy(v_hbm.at[p], v_ref.at[p], v_sem.at[p]) for p in range(2)]
    loads[0].start()
    for load in v_loads:
        load.start()
    loads[1].start()

    barrier = pltpu.get_barrier_semaphore()
    for peer in peers:
        pl.semaphore_signal(
            barrier, inc=1, device_id={"tile": peer}, device_id_type=pl.DeviceIdType.MESH
        )

    for b in range(batches):
        rows_ref[b, pl.ds(total, RMAX), :] = jnp.zeros((RMAX, LANES), f32)

    def copy_of(e, b, d):
        return pltpu.make_async_remote_copy(
            src_ref=send_ref.at[e, b, d],
            dst_ref=recv_ref.at[e, b, me],
            send_sem=send_sem.at[e, b],
            recv_sem=recv_sem.at[e, b],
            device_id={"tile": peers[d]},
            device_id_type=pl.DeviceIdType.MESH,
        )

    def all_of(e, b):
        return pltpu.make_async_remote_copy(
            src_ref=send_ref.at[e, b],
            dst_ref=recv_ref.at[e, b, pl.ds(0, n - 1)],
            send_sem=send_sem.at[e, b],
            recv_sem=recv_sem.at[e, b],
            device_id={"tile": peers[0]},
            device_id_type=pl.DeviceIdType.MESH,
        )

    def send_rows(e, b, side):
        def slot(k):
            return rows_ref[b, pl.ds(start_ref[side, k], RMAX), :].astype(bf16)

        for d, peer in enumerate(peers):
            send_ref[e, b, d] = slot(peer)
            copy_of(e, b, d).start()
        recv_ref[e, b, me] = slot(me)

    def join(e, b, side):
        all_of(e, b).wait_recv()
        for k in range(n):
            slots_ref[pl.ds(k * RMAX, RMAX), :] = recv_ref[e, b, k].astype(f32)
        row = lax.broadcasted_iota(jnp.int32, (8, LANES), 0)

        def group(k):
            first = slots_ref[pl.ds(table_ref[side, 0, k], 8), :]
            second = slots_ref[pl.ds(table_ref[side, 1, k], 8), :]
            return jnp.where(row < table_ref[side, 2, k], first, second)

        for k in range(0, blocks, 2):
            pair = jnp.concatenate([group(k), group(k + 1)], axis=0)
            joined_ref[pl.ds(k * 8, 16), :] = pair.astype(bf16)

    lane = lax.broadcasted_iota(jnp.int32, (width, sources), 1)
    loads[0].wait()
    xr, xi = x_ref[0], x_ref[1]
    turned_r, turned_i = pltpu.roll(xr, half, 1), pltpu.roll(xi, half, 1)
    low = lane < half
    xw_ref[0, :, :sources] = jnp.where(low, xr, turned_i).astype(bf16)
    xw_ref[0, :, sources:] = jnp.where(low, turned_r, xi).astype(bf16)
    xw_ref[1, :, :sources] = jnp.where(low, -xi, turned_r).astype(bf16)
    xw_ref[1, :, sources:] = jnp.where(low, -turned_i, xr).astype(bf16)
    v_loads[0].wait()
    value = jnp.dot(v_ref[0], xw_ref[0], preferred_element_type=f32)
    v_loads[1].wait()
    for load in loads[2:]:
        load.start()
    value = value + jnp.dot(v_ref[1], xw_ref[1], preferred_element_type=f32)
    for b in range(batches):
        rows_ref[b, pl.ds(0, total), :] = value[:, b * LANES : (b + 1) * LANES]
    loads[1].wait()
    row_start, column_start = 0, 0
    for k in range(n):
        start_ref[0, k] = row_start
        start_ref[1, k] = column_start
        row_start = row_start + rank_ref[me, k]
        column_start = column_start + rank_ref[k, me]
    pl.semaphore_wait(barrier, n - 1)
    for b in range(batches):
        send_rows(0, b, 1)

    for side in range(2):

        def entry(k, carry):
            tile, start = carry
            end = start + (rank_ref[me, tile] if side == 0 else rank_ref[tile, me])
            table_ref[side, 0, k] = jnp.clip(tile * RMAX + k * 8 - start, 0, n * RMAX)
            table_ref[side, 1, k] = jnp.clip((tile + 1) * RMAX + k * 8 - end, 0, n * RMAX)
            table_ref[side, 2, k] = end - k * 8
            leave = end <= k * 8 + 8
            later = jnp.minimum(tile + 1, n - 1)
            return jnp.where(leave, later, tile), jnp.where(leave, end, start)

        lax.fori_loop(0, blocks, entry, (jnp.int32(0), jnp.int32(0)))
    slots_ref[pl.ds(n * RMAX, 8), :] = jnp.zeros((8, LANES), f32)
    for p in range(2):
        turned = x_ref[p].T
        for b in range(batches):
            xt_ref[b, pl.ds(p * half, half), :] = turned[b * half : (b + 1) * half]
    for load in loads[2:]:
        load.wait()

    def field_of(b):
        c = joined_ref[...]
        p = dot_first(c, u_ref[0])
        q = dot_first(c, u_ref[1])
        yr = p[:half] - q[half:]
        yi = q[:half] + p[half:]
        rows = pl.ds(pl.multiple_of(b * half, half), half)
        hr = sums_ref[0, rows, :] * yr - sums_ref[1, rows, :] * yi - sums_ref[3, rows, :]
        hi = sums_ref[2, rows, :] * yi - sums_ref[1, rows, :] * yr + sums_ref[4, rows, :]
        return hr.astype(bf16), hi.astype(bf16)

    def step_model(b):
        a = joined_ref[...]
        p = dot_first(a, v_ref[0])
        q = dot_first(a, v_ref[1])
        xr = xt_ref[b, :half, :] - step_size * (p[:half] + q[half:])
        xi = xt_ref[b, half:, :] - step_size * (p[half:] - q[:half])
        return xr, xi

    for iteration in range(ITERS):
        e = 2 * iteration

        def residual_step(b, carry):
            if iteration == 0:
                first = b * half
                add_windows(record_ref, open_ref, close_ref, sums_ref, first, half)
            join(e, b, 0)
            hr, hi = field_of(b)
            rows_ref[b, pl.ds(0, total), :] = dot_last(
                u_ref[0], jnp.concatenate([hr, hi], axis=0)
            ) + dot_last(u_ref[1], jnp.concatenate([hi, -hr], axis=0))
            send_rows(e + 1, b, 0)
            return carry

        lax.fori_loop(0, batches, residual_step, 0)
        if iteration + 1 < ITERS:

            def model_step(b, carry):
                join(e + 1, b, 1)
                xr, xi = step_model(b)
                xt_ref[b, :half, :] = xr
                xt_ref[b, half:, :] = xi
                xr, xi = xr.astype(bf16), xi.astype(bf16)
                rows_ref[b, pl.ds(0, total), :] = dot_last(
                    v_ref[0], jnp.concatenate([xr, xi], axis=0)
                ) + dot_last(v_ref[1], jnp.concatenate([-xi, xr], axis=0))
                send_rows(e + 2, b, 1)
                return carry

            lax.fori_loop(0, batches, model_step, 0)
        else:
            for b in range(batches):
                join(e + 1, b, 1)
                xr, xi = step_model(b)
                out_ref[b, :half, :] = xr
                out_ref[b, half:, :] = xi

    def finish(e, carry):
        for b in range(batches):
            all_of(e, b).wait_send()
        return carry

    lax.fori_loop(0, 2 * ITERS, finish, 0)


def fused(start_model, v_basis, u_parts, records, ranks, window_start, window_stop):
    inputs = (ranks, start_model, v_basis, u_parts, records, window_start, window_stop)
    n = ranks.shape[0]
    _, width, sources = start_model.shape
    _, total, _ = v_basis.shape
    receivers = records.shape[2]
    exchanges, batches = 2 * ITERS, 2
    like = lambda a: pltpu.VMEM(a.shape, a.dtype)
    return pl.pallas_call(
        functools.partial(fused_kernel, n),
        out_shape=jax.ShapeDtypeStruct((batches, sources, width), f32),
        in_specs=[far] * 7,
        out_specs=near,
        scratch_shapes=[
            pltpu.SMEM(ranks.shape, ranks.dtype),
            like(start_model),
            like(v_basis),
            like(u_parts),
            like(records),
            like(window_start),
            like(window_stop),
            pltpu.VMEM((2, width, 2 * sources), bf16),
            pltpu.VMEM((batches, sources, width), f32),
            pltpu.VMEM((5, sources, receivers), f32),
            pltpu.VMEM((batches, total + RMAX, LANES), f32),
            pltpu.VMEM((n * RMAX + 8, LANES), f32),
            pltpu.VMEM((total, LANES), bf16),
            pltpu.VMEM((exchanges, batches, n - 1, RMAX, LANES), bf16),
            pltpu.VMEM((exchanges, batches, n, RMAX, LANES), bf16),
            pltpu.SMEM((2, n), jnp.int32),
            pltpu.SMEM((2, 3, total // 8), jnp.int32),
            pltpu.SemaphoreType.DMA((6,)),
            pltpu.SemaphoreType.DMA((2,)),
            pltpu.SemaphoreType.DMA((exchanges, batches)),
            pltpu.SemaphoreType.DMA((exchanges, batches)),
        ],
        compiler_params=pltpu.CompilerParams(
            collective_id=0, has_side_effects=True, vmem_limit_bytes=44 * 1024 * 1024
        ),
    )(*[pltpu.with_memory_space_constraint(a, pltpu.HBM) for a in inputs])


def turn_kernel(xt_ref, out_ref):
    batches, sources, _ = xt_ref.shape
    half = sources // batches
    _, rows, _ = out_ref.shape
    lanes = pl.ds(pl.multiple_of(pl.program_id(0) * rows, rows), rows)
    for p in range(2):
        part = [xt_ref[b, p * half : (p + 1) * half, lanes] for b in range(batches)]
        out_ref[p] = jnp.concatenate(part, axis=0).T


def by_row(xt):
    _, sources, width = xt.shape
    rows = width // PARTS
    return pl.pallas_call(
        turn_kernel,
        grid=(PARTS,),
        out_shape=jax.ShapeDtypeStruct((2, width, sources), xt.dtype),
        in_specs=[near],
        out_specs=pl.BlockSpec((2, rows, sources), lambda k: (0, k, 0)),
        compiler_params=pltpu.CompilerParams(vmem_limit_bytes=16 * 1024 * 1024),
    )(xt)


def on_device(start_model, v_basis, u_basis, records, tile_ranks, window_start, window_stop):
    n = lax.axis_size("tile")
    freq_count, rows_count, cols_count = tile_ranks.shape
    single = freq_count == 1 and n == rows_count and n == cols_count and n & (n - 1) == 0
    fits = start_model.shape[2] == LANES and v_basis.shape[1] % 16 == 0
    fits = fits and records.shape[2] % (4 * LANES) == 0 and start_model.shape[1] % LANES == 0
    if not (single and fits):
        return on_device_general(
            start_model, v_basis, u_basis, records, tile_ranks, window_start, window_stop
        )
    xt = fused(
        start_model, v_basis, u_basis[:, 0], records, tile_ranks[0], window_start, window_stop
    )
    return by_row(xt)


def solution(mesh):
    in_specs = (
        P(None, ("groups", "tile"), None),
        P(None, ("groups", "tile"), None),
        P(None, None, None, ("groups", "tile")),
        P(None, None, ("groups", "tile")),
        P("groups", None, None),
        P(None, ("groups", "tile")),
        P(None, ("groups", "tile")),
    )
    out_specs = P(None, ("groups", "tile"), None)
    return jax.shard_map(
        on_device, mesh=mesh, in_specs=in_specs, out_specs=out_specs, check_vma=False
    )
```

```python
import functools
import math

import jax
import jax.numpy as jnp
from jax import lax
from jax.experimental import pallas as pl
from jax.experimental.pallas import tpu as pltpu
from jax.sharding import PartitionSpec as P

RMAX = 96
ITERS = 2


step_size = 0.5
precise = lax.Precision.HIGHEST


def wave_tables(bin_count, sample_count):
    moments = jnp.arange(sample_count, dtype=jnp.float32)
    bin_ids = jnp.arange(bin_count, dtype=jnp.float32) + 1.0
    phases = 2.0 * math.pi / sample_count * bin_ids[:, None] * moments[None, :]
    factor = math.sqrt(2.0 / sample_count)
    return (jnp.cos(phases) * factor, jnp.sin(phases) * factor)


def piece_tree(partials, axis):
    current = partials
    while current.shape[axis] > 1:
        half_count = current.shape[axis] // 2
        lower_part = lax.slice_in_dim(current, 0, half_count, axis=axis).astype(jnp.float32)
        upper_part = lax.slice_in_dim(current, half_count, 2 * half_count, axis=axis).astype(
            jnp.float32
        )
        current = (lower_part + upper_part).astype(jnp.bfloat16)
    return jnp.squeeze(current, axis)


def starts_along(tile_ranks, axis):
    count = tile_ranks.shape[axis]
    return jnp.concatenate(
        [
            jnp.sum(lax.slice_in_dim(tile_ranks, 0, k, axis=axis), axis=axis, keepdims=True)
            for k in range(count)
        ],
        axis=axis,
    ).astype(jnp.int32)


def pack_slots(source_rows, rank_each, start_each):
    padded = jnp.pad(source_rows, ((0, 0), (0, RMAX), (0, 0)))
    live = jnp.arange(RMAX, dtype=jnp.int32)[None, :, None]

    def cut(operands):
        rank, start = operands
        rows = lax.dynamic_slice_in_dim(padded, start, RMAX, axis=1)
        return jnp.where(live < rank, rows, jnp.zeros((), rows.dtype))

    return jnp.moveaxis(lax.map(cut, (rank_each, start_each)), 0, 1)


def join_slots(slots, starts, total):
    joined = jnp.zeros((slots.shape[0], total + RMAX, slots.shape[3]), slots.dtype)

    def place(k, joined):
        rows = lax.dynamic_index_in_dim(slots, k, 1, False)
        return lax.dynamic_update_slice_in_dim(joined, rows, starts[k], axis=1)

    return lax.fori_loop(0, slots.shape[1], place, joined)[:, :total]


def on_device_general(start_model, v_basis, u_basis, records, tile_ranks, window_start, window_stop):
    tile_count = lax.axis_size("tile")
    device = lax.axis_index("tile")
    freq_count, rows_count, cols_count = tile_ranks.shape
    rank_total = v_basis.shape[1]
    pieces = tile_count // rows_count
    my_freq = device // cols_count
    my_col = device % cols_count
    my_row = device // pieces
    down_offsets = starts_along(tile_ranks, 1)
    side_offsets = starts_along(tile_ranks, 2)
    column_ranks = lax.dynamic_index_in_dim(
        lax.dynamic_index_in_dim(tile_ranks, my_freq, 0, False), my_col, 1, False
    )
    column_starts = lax.dynamic_index_in_dim(
        lax.dynamic_index_in_dim(down_offsets, my_freq, 0, False), my_col, 1, False
    )
    row_ranks = lax.dynamic_index_in_dim(tile_ranks, my_row, 1, False)
    row_starts = lax.dynamic_index_in_dim(side_offsets, my_row, 1, False)
    fwd_rank = jnp.broadcast_to(column_ranks[:, None], (rows_count, pieces)).reshape(tile_count)
    fwd_start = jnp.broadcast_to(column_starts[:, None], (rows_count, pieces)).reshape(tile_count)
    dest_freq = jnp.arange(tile_count, dtype=jnp.int32) // cols_count
    adj_rank = row_ranks.reshape(tile_count)
    adj_start = row_starts.reshape(tile_count) + dest_freq * rank_total
    cos_table, sin_table = wave_tables(freq_count, records.shape[0])
    moments = jnp.arange(records.shape[0], dtype=jnp.int32)[:, None, None]
    inside = (moments >= window_start[None]) & (moments < window_stop[None])
    observed = records.astype(jnp.float32)
    current = start_model
    for iteration in range(ITERS):
        rounded = current.astype(jnp.bfloat16)
        coeff_real = jnp.dot(v_basis[0], rounded[0], preferred_element_type=jnp.float32) - jnp.dot(
            v_basis[1], rounded[1], preferred_element_type=jnp.float32
        )
        coeff_imag = jnp.dot(v_basis[0], rounded[1], preferred_element_type=jnp.float32) + jnp.dot(
            v_basis[1], rounded[0], preferred_element_type=jnp.float32
        )
        coefficients = jnp.stack([coeff_real, coeff_imag]).astype(jnp.bfloat16)
        outbound = pack_slots(coefficients, fwd_rank, fwd_start)
        forward_received = lax.all_to_all(outbound, "tile", split_axis=1, concat_axis=1, tiled=True)
        grouped_cols = forward_received.reshape(
            2, freq_count, cols_count, RMAX, forward_received.shape[3]
        )
        forward_chosen = jnp.stack(
            [join_slots(grouped_cols[:, f], row_starts[f], rank_total) for f in range(freq_count)],
            axis=1,
        )
        pred_real = jnp.einsum(
            "fks,fkn->fsn", forward_chosen[0], u_basis[0], preferred_element_type=jnp.float32
        ) - jnp.einsum(
            "fks,fkn->fsn", forward_chosen[1], u_basis[1], preferred_element_type=jnp.float32
        )
        pred_imag = jnp.einsum(
            "fks,fkn->fsn", forward_chosen[0], u_basis[1], preferred_element_type=jnp.float32
        ) + jnp.einsum(
            "fks,fkn->fsn", forward_chosen[1], u_basis[0], preferred_element_type=jnp.float32
        )
        predicted = jnp.stack([pred_real, pred_imag])
        traces = jnp.einsum("ft,fsn->tsn", cos_table, predicted[0], precision=precise) - jnp.einsum(
            "ft,fsn->tsn", sin_table, predicted[1], precision=precise
        )
        residual = jnp.where(inside, traces - observed, jnp.zeros((), jnp.float32))
        back_real = jnp.einsum("ft,tsn->fsn", cos_table, residual, precision=precise)
        back_imag = -jnp.einsum("ft,tsn->fsn", sin_table, residual, precision=precise)
        adjoint_field = jnp.stack([back_real, back_imag]).astype(jnp.bfloat16)
        part_real = jnp.einsum(
            "fkn,fsn->fks", u_basis[0], adjoint_field[0], preferred_element_type=jnp.float32
        ) + jnp.einsum(
            "fkn,fsn->fks", u_basis[1], adjoint_field[1], preferred_element_type=jnp.float32
        )
        part_imag = jnp.einsum(
            "fkn,fsn->fks", u_basis[0], adjoint_field[1], preferred_element_type=jnp.float32
        ) - jnp.einsum(
            "fkn,fsn->fks", u_basis[1], adjoint_field[0], preferred_element_type=jnp.float32
        )
        partial_value = jnp.stack([part_real, part_imag]).astype(jnp.bfloat16)
        flat_partial = partial_value.reshape(2, freq_count * rank_total, partial_value.shape[3])
        outgoing = pack_slots(flat_partial, adj_rank, adj_start)
        received = lax.all_to_all(outgoing, "tile", split_axis=1, concat_axis=1, tiled=True)
        grouped_rows = received.reshape(2, rows_count, pieces, RMAX, received.shape[3])
        adjoint_summed = piece_tree(grouped_rows, 2)
        chosen = join_slots(adjoint_summed, column_starts, rank_total)
        contract_dims = (((0,), (0,)), ((), ()))
        grad_real = lax.dot_general(
            v_basis[0], chosen[0], contract_dims, preferred_element_type=jnp.float32
        ) + lax.dot_general(
            v_basis[1], chosen[1], contract_dims, preferred_element_type=jnp.float32
        )
        grad_imag = lax.dot_general(
            v_basis[0], chosen[1], contract_dims, preferred_element_type=jnp.float32
        ) - lax.dot_general(
            v_basis[1], chosen[0], contract_dims, preferred_element_type=jnp.float32
        )
        gradient = jnp.stack([grad_real, grad_imag])
        current = current - step_size * gradient
    return current


LANES = 128
PARTS = 2
f32 = jnp.float32
bf16 = jnp.bfloat16
far = pl.BlockSpec(memory_space=pltpu.HBM)
near = pl.BlockSpec(memory_space=pltpu.VMEM)


def dot_last(a, b):
    return lax.dot_general(a, b, (((1,), (1,)), ((), ())), preferred_element_type=f32)


def dot_first(a, b):
    return lax.dot_general(a, b, (((0,), (0,)), ((), ())), preferred_element_type=f32)


def xor_peer(me, mask, n):
    peer = me
    bit = 1
    while bit < n:
        if mask & bit:
            peer = peer + bit * (1 - 2 * ((me // bit) % 2))
        bit *= 2
    return peer


def add_windows(record_ref, open_ref, close_ref, sums_ref, first, count):
    sample_count = record_ref.shape[0]
    scale = math.sqrt(2.0 / sample_count)
    step, strip = 16, 4 * LANES
    strips = record_ref.shape[2] // strip

    def block(k, carry):
        rows = pl.ds(pl.multiple_of(first + (k // strips) * step, step), step)
        lanes = pl.ds(pl.multiple_of((k % strips) * strip, strip), strip)
        opened = open_ref[rows, lanes]
        closed = close_ref[rows, lanes]
        sums = [jnp.zeros(opened.shape, f32)] * 5
        for t in range(sample_count - 1):
            phase = 2.0 * math.pi / sample_count * t
            c, s = math.cos(phase) * scale, math.sin(phase) * scale
            seen = record_ref[t, rows, lanes].astype(f32)
            squares = (c * c, c * s, s * s)
            if sample_count // 4 <= t < sample_count // 2:
                terms = list(squares)
            else:
                inside = (t >= opened) if t < sample_count // 4 else (t < closed)
                seen = jnp.where(inside, seen, 0.0)
                terms = [jnp.where(inside, w, 0.0) for w in squares]
            terms += [seen * c, seen * s]
            sums = [x + y for x, y in zip(sums, terms)]
        for m in range(5):
            sums_ref[m, rows, lanes] = sums[m]
        return carry

    lax.fori_loop(0, (count // step) * strips, block, 0)


def fused_kernel(
    n, rank_hbm, x_hbm, v_hbm, u_hbm, record_hbm, open_hbm, close_hbm, out_ref,
    rank_ref, x_ref, v_ref, u_ref, record_ref, open_ref, close_ref,
    xw_ref, xt_ref, sums_ref, rows_ref, slots_ref, joined_ref, send_ref, recv_ref,
    start_ref, table_ref, load_sem, v_sem, send_sem, recv_sem,
):
    me = lax.axis_index("tile")
    q = n // 4
    masks = [m for k in (2, 1, 3) for m in range(k * q, (k + 1) * q)] + list(range(q - 1, 0, -1))
    peers = [xor_peer(me, mask, n) for mask in masks]
    _, total, width = v_ref.shape
    sources = x_ref.shape[2]
    half = sources // 2
    batches = 2
    blocks = total // 8

    loads = [
        pltpu.make_async_copy(source, target, load_sem.at[k])
        for k, (source, target) in enumerate(
            [
                (x_hbm, x_ref),
                (rank_hbm, rank_ref),
                (open_hbm, open_ref),
                (close_hbm, close_ref),
                (record_hbm, record_ref),
                (u_hbm, u_ref),
            ]
        )
    ]
    v_loads = [pltpu.make_async_copy(v_hbm.at[p], v_ref.at[p], v_sem.at[p]) for p in range(2)]
    loads[0].start()
    for load in v_loads:
        load.start()
    loads[1].start()

    barrier = pltpu.get_barrier_semaphore()
    for peer in peers:
        pl.semaphore_signal(
            barrier, inc=1, device_id={"tile": peer}, device_id_type=pl.DeviceIdType.MESH
        )

    for b in range(batches):
        rows_ref[b, pl.ds(total, RMAX), :] = jnp.zeros((RMAX, LANES), f32)

    def copy_of(e, b, d):
        return pltpu.make_async_remote_copy(
            src_ref=send_ref.at[e, b, d],
            dst_ref=recv_ref.at[e, b, me],
            send_sem=send_sem.at[e, b],
            recv_sem=recv_sem.at[e, b],
            device_id={"tile": peers[d]},
            device_id_type=pl.DeviceIdType.MESH,
        )

    def all_of(e, b):
        return pltpu.make_async_remote_copy(
            src_ref=send_ref.at[e, b],
            dst_ref=recv_ref.at[e, b, pl.ds(0, n - 1)],
            send_sem=send_sem.at[e, b],
            recv_sem=recv_sem.at[e, b],
            device_id={"tile": peers[0]},
            device_id_type=pl.DeviceIdType.MESH,
        )

    def send_rows(e, b, side):
        def slot(k):
            return rows_ref[b, pl.ds(start_ref[side, k], RMAX), :].astype(bf16)

        for d, peer in enumerate(peers):
            send_ref[e, b, d] = slot(peer)
            copy_of(e, b, d).start()
        recv_ref[e, b, me] = slot(me)

    def join(e, b, side):
        all_of(e, b).wait_recv()
        for k in range(n):
            slots_ref[pl.ds(k * RMAX, RMAX), :] = recv_ref[e, b, k].astype(f32)
        row = lax.broadcasted_iota(jnp.int32, (8, LANES), 0)

        def group(k):
            first = slots_ref[pl.ds(table_ref[side, 0, k], 8), :]
            second = slots_ref[pl.ds(table_ref[side, 1, k], 8), :]
            return jnp.where(row < table_ref[side, 2, k], first, second)

        for k in range(0, blocks, 2):
            pair = jnp.concatenate([group(k), group(k + 1)], axis=0)
            joined_ref[pl.ds(k * 8, 16), :] = pair.astype(bf16)

    lane = lax.broadcasted_iota(jnp.int32, (width, sources), 1)
    loads[0].wait()
    xr, xi = x_ref[0], x_ref[1]
    turned_r, turned_i = pltpu.roll(xr, half, 1), pltpu.roll(xi, half, 1)
    low = lane < half
    xw_ref[0, :, :sources] = jnp.where(low, xr, turned_i).astype(bf16)
    xw_ref[0, :, sources:] = jnp.where(low, turned_r, xi).astype(bf16)
    xw_ref[1, :, :sources] = jnp.where(low, -xi, turned_r).astype(bf16)
    xw_ref[1, :, sources:] = jnp.where(low, -turned_i, xr).astype(bf16)
    v_loads[0].wait()
    value = jnp.dot(v_ref[0], xw_ref[0], preferred_element_type=f32)
    v_loads[1].wait()
    for load in loads[2:]:
        load.start()
    value = value + jnp.dot(v_ref[1], xw_ref[1], preferred_element_type=f32)
    for b in range(batches):
        rows_ref[b, pl.ds(0, total), :] = value[:, b * LANES : (b + 1) * LANES]
    loads[1].wait()
    row_start, column_start = 0, 0
    for k in range(n):
        start_ref[0, k] = row_start
        start_ref[1, k] = column_start
        row_start = row_start + rank_ref[me, k]
        column_start = column_start + rank_ref[k, me]
    pl.semaphore_wait(barrier, n - 1)
    for b in range(batches):
        send_rows(0, b, 1)

    for side in range(2):

        def entry(k, carry):
            tile, start = carry
            end = start + (rank_ref[me, tile] if side == 0 else rank_ref[tile, me])
            table_ref[side, 0, k] = jnp.clip(tile * RMAX + k * 8 - start, 0, n * RMAX)
            table_ref[side, 1, k] = jnp.clip((tile + 1) * RMAX + k * 8 - end, 0, n * RMAX)
            table_ref[side, 2, k] = end - k * 8
            leave = end <= k * 8 + 8
            later = jnp.minimum(tile + 1, n - 1)
            return jnp.where(leave, later, tile), jnp.where(leave, end, start)

        lax.fori_loop(0, blocks, entry, (jnp.int32(0), jnp.int32(0)))
    slots_ref[pl.ds(n * RMAX, 8), :] = jnp.zeros((8, LANES), f32)
    for p in range(2):
        turned = x_ref[p].T
        for b in range(batches):
            xt_ref[b, pl.ds(p * half, half), :] = turned[b * half : (b + 1) * half]
    for load in loads[2:]:
        load.wait()

    def field_of(b):
        c = joined_ref[...]
        p = dot_first(c, u_ref[0])
        q = dot_first(c, u_ref[1])
        yr = p[:half] - q[half:]
        yi = q[:half] + p[half:]
        rows = pl.ds(pl.multiple_of(b * half, half), half)
        hr = sums_ref[0, rows, :] * yr - sums_ref[1, rows, :] * yi - sums_ref[3, rows, :]
        hi = sums_ref[2, rows, :] * yi - sums_ref[1, rows, :] * yr + sums_ref[4, rows, :]
        return hr.astype(bf16), hi.astype(bf16)

    def step_model(b):
        a = joined_ref[...]
        p = dot_first(a, v_ref[0])
        q = dot_first(a, v_ref[1])
        xr = xt_ref[b, :half, :] - step_size * (p[:half] + q[half:])
        xi = xt_ref[b, half:, :] - step_size * (p[half:] - q[:half])
        return xr, xi

    for iteration in range(ITERS):
        e = 2 * iteration

        def residual_step(b, carry):
            if iteration == 0:
                first = b * half
                add_windows(record_ref, open_ref, close_ref, sums_ref, first, half)
            join(e, b, 0)
            hr, hi = field_of(b)
            rows_ref[b, pl.ds(0, total), :] = dot_last(
                u_ref[0], jnp.concatenate([hr, hi], axis=0)
            ) + dot_last(u_ref[1], jnp.concatenate([hi, -hr], axis=0))
            send_rows(e + 1, b, 0)
            return carry

        lax.fori_loop(0, batches, residual_step, 0)
        if iteration + 1 < ITERS:

            def model_step(b, carry):
                join(e + 1, b, 1)
                xr, xi = step_model(b)
                xt_ref[b, :half, :] = xr
                xt_ref[b, half:, :] = xi
                xr, xi = xr.astype(bf16), xi.astype(bf16)
                rows_ref[b, pl.ds(0, total), :] = dot_last(
                    v_ref[0], jnp.concatenate([xr, xi], axis=0)
                ) + dot_last(v_ref[1], jnp.concatenate([-xi, xr], axis=0))
                send_rows(e + 2, b, 1)
                return carry

            lax.fori_loop(0, batches, model_step, 0)
        else:
            for b in range(batches):
                join(e + 1, b, 1)
                xr, xi = step_model(b)
                out_ref[b, :half, :] = xr
                out_ref[b, half:, :] = xi

    def finish(e, carry):
        for b in range(batches):
            all_of(e, b).wait_send()
        return carry

    lax.fori_loop(0, 2 * ITERS, finish, 0)


def fused(start_model, v_basis, u_parts, records, ranks, window_start, window_stop):
    inputs = (ranks, start_model, v_basis, u_parts, records, window_start, window_stop)
    n = ranks.shape[0]
    _, width, sources = start_model.shape
    _, total, _ = v_basis.shape
    receivers = records.shape[2]
    exchanges, batches = 2 * ITERS, 2
    like = lambda a: pltpu.VMEM(a.shape, a.dtype)
    return pl.pallas_call(
        functools.partial(fused_kernel, n),
        out_shape=jax.ShapeDtypeStruct((batches, sources, width), f32),
        in_specs=[far] * 7,
        out_specs=near,
        scratch_shapes=[
            pltpu.SMEM(ranks.shape, ranks.dtype),
            like(start_model),
            like(v_basis),
            like(u_parts),
            like(records),
            like(window_start),
            like(window_stop),
            pltpu.VMEM((2, width, 2 * sources), bf16),
            pltpu.VMEM((batches, sources, width), f32),
            pltpu.VMEM((5, sources, receivers), f32),
            pltpu.VMEM((batches, total + RMAX, LANES), f32),
            pltpu.VMEM((n * RMAX + 8, LANES), f32),
            pltpu.VMEM((total, LANES), bf16),
            pltpu.VMEM((exchanges, batches, n - 1, RMAX, LANES), bf16),
            pltpu.VMEM((exchanges, batches, n, RMAX, LANES), bf16),
            pltpu.SMEM((2, n), jnp.int32),
            pltpu.SMEM((2, 3, total // 8), jnp.int32),
            pltpu.SemaphoreType.DMA((6,)),
            pltpu.SemaphoreType.DMA((2,)),
            pltpu.SemaphoreType.DMA((exchanges, batches)),
            pltpu.SemaphoreType.DMA((exchanges, batches)),
        ],
        compiler_params=pltpu.CompilerParams(
            collective_id=0, has_side_effects=True, vmem_limit_bytes=44 * 1024 * 1024
        ),
    )(*[pltpu.with_memory_space_constraint(a, pltpu.HBM) for a in inputs])


def turn_kernel(xt_ref, out_ref):
    batches, sources, _ = xt_ref.shape
    half = sources // batches
    _, rows, _ = out_ref.shape
    lanes = pl.ds(pl.multiple_of(pl.program_id(0) * rows, rows), rows)
    for p in range(2):
        part = [xt_ref[b, p * half : (p + 1) * half, lanes] for b in range(batches)]
        out_ref[p] = jnp.concatenate(part, axis=0).T


def by_row(xt):
    _, sources, width = xt.shape
    rows = width // PARTS
    return pl.pallas_call(
        turn_kernel,
        grid=(PARTS,),
        out_shape=jax.ShapeDtypeStruct((2, width, sources), xt.dtype),
        in_specs=[near],
        out_specs=pl.BlockSpec((2, rows, sources), lambda k: (0, k, 0)),
        compiler_params=pltpu.CompilerParams(vmem_limit_bytes=16 * 1024 * 1024),
    )(xt)


def on_device(start_model, v_basis, u_basis, records, tile_ranks, window_start, window_stop):
    n = lax.axis_size("tile")
    freq_count, rows_count, cols_count = tile_ranks.shape
    single = freq_count == 1 and n == rows_count and n == cols_count and n >= 4 and n & (n - 1) == 0
    fits = start_model.shape[2] == LANES and v_basis.shape[1] % 16 == 0
    fits = fits and records.shape[2] % (4 * LANES) == 0 and start_model.shape[1] % LANES == 0
    if not (single and fits):
        return on_device_general(
            start_model, v_basis, u_basis, records, tile_ranks, window_start, window_stop
        )
    xt = fused(
        start_model, v_basis, u_basis[:, 0], records, tile_ranks[0], window_start, window_stop
    )
    return by_row(xt)


def solution(mesh):
    in_specs = (
        P(None, ("groups", "tile"), None),
        P(None, ("groups", "tile"), None),
        P(None, None, None, ("groups", "tile")),
        P(None, None, ("groups", "tile")),
        P("groups", None, None),
        P(None, ("groups", "tile")),
        P(None, ("groups", "tile")),
    )
    out_specs = P(None, ("groups", "tile"), None)
    return jax.shard_map(
        on_device, mesh=mesh, in_specs=in_specs, out_specs=out_specs, check_vma=False
    )
```

```python
import functools
import math

import jax
import jax.numpy as jnp
from jax import lax
from jax.experimental import pallas as pl
from jax.experimental.pallas import tpu as pltpu
from jax.sharding import PartitionSpec as P

RMAX = 96
ITERS = 2


step_size = 0.5
precise = lax.Precision.HIGHEST


def wave_tables(bin_count, sample_count):
    moments = jnp.arange(sample_count, dtype=jnp.float32)
    bin_ids = jnp.arange(bin_count, dtype=jnp.float32) + 1.0
    phases = 2.0 * math.pi / sample_count * bin_ids[:, None] * moments[None, :]
    factor = math.sqrt(2.0 / sample_count)
    return (jnp.cos(phases) * factor, jnp.sin(phases) * factor)


def piece_tree(partials, axis):
    current = partials
    while current.shape[axis] > 1:
        half_count = current.shape[axis] // 2
        lower_part = lax.slice_in_dim(current, 0, half_count, axis=axis).astype(jnp.float32)
        upper_part = lax.slice_in_dim(current, half_count, 2 * half_count, axis=axis).astype(
            jnp.float32
        )
        current = (lower_part + upper_part).astype(jnp.bfloat16)
    return jnp.squeeze(current, axis)


def starts_along(tile_ranks, axis):
    count = tile_ranks.shape[axis]
    return jnp.concatenate(
        [
            jnp.sum(lax.slice_in_dim(tile_ranks, 0, k, axis=axis), axis=axis, keepdims=True)
            for k in range(count)
        ],
        axis=axis,
    ).astype(jnp.int32)


def pack_slots(source_rows, rank_each, start_each):
    padded = jnp.pad(source_rows, ((0, 0), (0, RMAX), (0, 0)))
    live = jnp.arange(RMAX, dtype=jnp.int32)[None, :, None]

    def cut(operands):
        rank, start = operands
        rows = lax.dynamic_slice_in_dim(padded, start, RMAX, axis=1)
        return jnp.where(live < rank, rows, jnp.zeros((), rows.dtype))

    return jnp.moveaxis(lax.map(cut, (rank_each, start_each)), 0, 1)


def join_slots(slots, starts, total):
    joined = jnp.zeros((slots.shape[0], total + RMAX, slots.shape[3]), slots.dtype)

    def place(k, joined):
        rows = lax.dynamic_index_in_dim(slots, k, 1, False)
        return lax.dynamic_update_slice_in_dim(joined, rows, starts[k], axis=1)

    return lax.fori_loop(0, slots.shape[1], place, joined)[:, :total]


def on_device_general(start_model, v_basis, u_basis, records, tile_ranks, window_start, window_stop):
    tile_count = lax.axis_size("tile")
    device = lax.axis_index("tile")
    freq_count, rows_count, cols_count = tile_ranks.shape
    rank_total = v_basis.shape[1]
    pieces = tile_count // rows_count
    my_freq = device // cols_count
    my_col = device % cols_count
    my_row = device // pieces
    down_offsets = starts_along(tile_ranks, 1)
    side_offsets = starts_along(tile_ranks, 2)
    column_ranks = lax.dynamic_index_in_dim(
        lax.dynamic_index_in_dim(tile_ranks, my_freq, 0, False), my_col, 1, False
    )
    column_starts = lax.dynamic_index_in_dim(
        lax.dynamic_index_in_dim(down_offsets, my_freq, 0, False), my_col, 1, False
    )
    row_ranks = lax.dynamic_index_in_dim(tile_ranks, my_row, 1, False)
    row_starts = lax.dynamic_index_in_dim(side_offsets, my_row, 1, False)
    fwd_rank = jnp.broadcast_to(column_ranks[:, None], (rows_count, pieces)).reshape(tile_count)
    fwd_start = jnp.broadcast_to(column_starts[:, None], (rows_count, pieces)).reshape(tile_count)
    dest_freq = jnp.arange(tile_count, dtype=jnp.int32) // cols_count
    adj_rank = row_ranks.reshape(tile_count)
    adj_start = row_starts.reshape(tile_count) + dest_freq * rank_total
    cos_table, sin_table = wave_tables(freq_count, records.shape[0])
    moments = jnp.arange(records.shape[0], dtype=jnp.int32)[:, None, None]
    inside = (moments >= window_start[None]) & (moments < window_stop[None])
    observed = records.astype(jnp.float32)
    current = start_model
    for iteration in range(ITERS):
        rounded = current.astype(jnp.bfloat16)
        coeff_real = jnp.dot(v_basis[0], rounded[0], preferred_element_type=jnp.float32) - jnp.dot(
            v_basis[1], rounded[1], preferred_element_type=jnp.float32
        )
        coeff_imag = jnp.dot(v_basis[0], rounded[1], preferred_element_type=jnp.float32) + jnp.dot(
            v_basis[1], rounded[0], preferred_element_type=jnp.float32
        )
        coefficients = jnp.stack([coeff_real, coeff_imag]).astype(jnp.bfloat16)
        outbound = pack_slots(coefficients, fwd_rank, fwd_start)
        forward_received = lax.all_to_all(outbound, "tile", split_axis=1, concat_axis=1, tiled=True)
        grouped_cols = forward_received.reshape(
            2, freq_count, cols_count, RMAX, forward_received.shape[3]
        )
        forward_chosen = jnp.stack(
            [join_slots(grouped_cols[:, f], row_starts[f], rank_total) for f in range(freq_count)],
            axis=1,
        )
        pred_real = jnp.einsum(
            "fks,fkn->fsn", forward_chosen[0], u_basis[0], preferred_element_type=jnp.float32
        ) - jnp.einsum(
            "fks,fkn->fsn", forward_chosen[1], u_basis[1], preferred_element_type=jnp.float32
        )
        pred_imag = jnp.einsum(
            "fks,fkn->fsn", forward_chosen[0], u_basis[1], preferred_element_type=jnp.float32
        ) + jnp.einsum(
            "fks,fkn->fsn", forward_chosen[1], u_basis[0], preferred_element_type=jnp.float32
        )
        predicted = jnp.stack([pred_real, pred_imag])
        traces = jnp.einsum("ft,fsn->tsn", cos_table, predicted[0], precision=precise) - jnp.einsum(
            "ft,fsn->tsn", sin_table, predicted[1], precision=precise
        )
        residual = jnp.where(inside, traces - observed, jnp.zeros((), jnp.float32))
        back_real = jnp.einsum("ft,tsn->fsn", cos_table, residual, precision=precise)
        back_imag = -jnp.einsum("ft,tsn->fsn", sin_table, residual, precision=precise)
        adjoint_field = jnp.stack([back_real, back_imag]).astype(jnp.bfloat16)
        part_real = jnp.einsum(
            "fkn,fsn->fks", u_basis[0], adjoint_field[0], preferred_element_type=jnp.float32
        ) + jnp.einsum(
            "fkn,fsn->fks", u_basis[1], adjoint_field[1], preferred_element_type=jnp.float32
        )
        part_imag = jnp.einsum(
            "fkn,fsn->fks", u_basis[0], adjoint_field[1], preferred_element_type=jnp.float32
        ) - jnp.einsum(
            "fkn,fsn->fks", u_basis[1], adjoint_field[0], preferred_element_type=jnp.float32
        )
        partial_value = jnp.stack([part_real, part_imag]).astype(jnp.bfloat16)
        flat_partial = partial_value.reshape(2, freq_count * rank_total, partial_value.shape[3])
        outgoing = pack_slots(flat_partial, adj_rank, adj_start)
        received = lax.all_to_all(outgoing, "tile", split_axis=1, concat_axis=1, tiled=True)
        grouped_rows = received.reshape(2, rows_count, pieces, RMAX, received.shape[3])
        adjoint_summed = piece_tree(grouped_rows, 2)
        chosen = join_slots(adjoint_summed, column_starts, rank_total)
        contract_dims = (((0,), (0,)), ((), ()))
        grad_real = lax.dot_general(
            v_basis[0], chosen[0], contract_dims, preferred_element_type=jnp.float32
        ) + lax.dot_general(
            v_basis[1], chosen[1], contract_dims, preferred_element_type=jnp.float32
        )
        grad_imag = lax.dot_general(
            v_basis[0], chosen[1], contract_dims, preferred_element_type=jnp.float32
        ) - lax.dot_general(
            v_basis[1], chosen[0], contract_dims, preferred_element_type=jnp.float32
        )
        gradient = jnp.stack([grad_real, grad_imag])
        current = current - step_size * gradient
    return current


LANES = 128
f32 = jnp.float32
bf16 = jnp.bfloat16
far = pl.BlockSpec(memory_space=pltpu.HBM)
near = pl.BlockSpec(memory_space=pltpu.VMEM)


def dot_last(a, b):
    return lax.dot_general(a, b, (((1,), (1,)), ((), ())), preferred_element_type=f32)


def dot_first(a, b):
    return lax.dot_general(a, b, (((0,), (0,)), ((), ())), preferred_element_type=f32)


def xor_peer(me, mask, n):
    peer = me
    bit = 1
    while bit < n:
        if mask & bit:
            peer = peer + bit * (1 - 2 * ((me // bit) % 2))
        bit *= 2
    return peer


def add_windows(record_ref, open_ref, close_ref, sums_ref, first, count):
    sample_count = record_ref.shape[0]
    scale = math.sqrt(2.0 / sample_count)
    step, strip = 16, 4 * LANES
    strips = record_ref.shape[2] // strip

    def block(k, carry):
        rows = pl.ds(pl.multiple_of(first + (k // strips) * step, step), step)
        lanes = pl.ds(pl.multiple_of((k % strips) * strip, strip), strip)
        opened = open_ref[rows, lanes]
        closed = close_ref[rows, lanes]
        sums = [jnp.zeros(opened.shape, f32)] * 5
        for t in range(sample_count - 1):
            phase = 2.0 * math.pi / sample_count * t
            c, s = math.cos(phase) * scale, math.sin(phase) * scale
            seen = record_ref[t, rows, lanes].astype(f32)
            squares = (c * c, c * s, s * s)
            if sample_count // 4 <= t < sample_count // 2:
                terms = list(squares)
            else:
                inside = (t >= opened) if t < sample_count // 4 else (t < closed)
                seen = jnp.where(inside, seen, 0.0)
                terms = [jnp.where(inside, w, 0.0) for w in squares]
            terms += [seen * c, seen * s]
            sums = [x + y for x, y in zip(sums, terms)]
        for m in range(5):
            sums_ref[m, rows, lanes] = sums[m]
        return carry

    lax.fori_loop(0, (count // step) * strips, block, 0)


def fused_kernel(
    n, rank_hbm, x_hbm, v_hbm, u_hbm, record_hbm, open_hbm, close_hbm, out_ref,
    rank_ref, x_ref, v_ref, u_ref, record_ref, open_ref, close_ref,
    xw_ref, xt_ref, sums_ref, rows_ref, slots_ref, joined_ref, send_ref, recv_ref,
    start_ref, table_ref, load_sem, v_sem, send_sem, recv_sem,
):
    me = lax.axis_index("tile")
    q = n // 4
    masks = [m for k in (2, 1, 3) for m in range(k * q, (k + 1) * q)] + list(range(q - 1, 0, -1))
    peers = [xor_peer(me, mask, n) for mask in masks]
    _, total, width = v_ref.shape
    sources = x_ref.shape[2]
    half = sources // 2
    batches = 2
    blocks = total // 8

    loads = [
        pltpu.make_async_copy(source, target, load_sem.at[k])
        for k, (source, target) in enumerate(
            [
                (x_hbm, x_ref),
                (rank_hbm, rank_ref),
                (open_hbm, open_ref),
                (close_hbm, close_ref),
                (record_hbm, record_ref),
                (u_hbm, u_ref),
            ]
        )
    ]
    v_loads = [pltpu.make_async_copy(v_hbm.at[p], v_ref.at[p], v_sem.at[p]) for p in range(2)]
    loads[0].start()
    for load in v_loads:
        load.start()
    loads[1].start()

    barrier = pltpu.get_barrier_semaphore()
    for peer in peers:
        pl.semaphore_signal(
            barrier, inc=1, device_id={"tile": peer}, device_id_type=pl.DeviceIdType.MESH
        )

    for b in range(batches):
        rows_ref[b, pl.ds(total, RMAX), :] = jnp.zeros((RMAX, LANES), f32)

    def copy_of(e, b, d):
        return pltpu.make_async_remote_copy(
            src_ref=send_ref.at[e, b, d],
            dst_ref=recv_ref.at[e, b, me],
            send_sem=send_sem.at[e, b],
            recv_sem=recv_sem.at[e, b],
            device_id={"tile": peers[d]},
            device_id_type=pl.DeviceIdType.MESH,
        )

    def all_of(e, b):
        return pltpu.make_async_remote_copy(
            src_ref=send_ref.at[e, b],
            dst_ref=recv_ref.at[e, b, pl.ds(0, n - 1)],
            send_sem=send_sem.at[e, b],
            recv_sem=recv_sem.at[e, b],
            device_id={"tile": peers[0]},
            device_id_type=pl.DeviceIdType.MESH,
        )

    def send_rows(e, b, side):
        def slot(k):
            return rows_ref[b, pl.ds(start_ref[side, k], RMAX), :].astype(bf16)

        for d, peer in enumerate(peers):
            send_ref[e, b, d] = slot(peer)
            copy_of(e, b, d).start()
        recv_ref[e, b, me] = slot(me)

    def join(e, b, side):
        all_of(e, b).wait_recv()
        for k in range(n):
            slots_ref[pl.ds(k * RMAX, RMAX), :] = recv_ref[e, b, k].astype(f32)
        row = lax.broadcasted_iota(jnp.int32, (8, LANES), 0)

        def group(k):
            first = slots_ref[pl.ds(table_ref[side, 0, k], 8), :]
            second = slots_ref[pl.ds(table_ref[side, 1, k], 8), :]
            return jnp.where(row < table_ref[side, 2, k], first, second)

        for k in range(0, blocks, 2):
            pair = jnp.concatenate([group(k), group(k + 1)], axis=0)
            joined_ref[pl.ds(k * 8, 16), :] = pair.astype(bf16)

    lane = lax.broadcasted_iota(jnp.int32, (width, sources), 1)
    loads[0].wait()
    xr, xi = x_ref[0], x_ref[1]
    turned_r, turned_i = pltpu.roll(xr, half, 1), pltpu.roll(xi, half, 1)
    low = lane < half
    xw_ref[0, :, :sources] = jnp.where(low, xr, turned_i).astype(bf16)
    xw_ref[0, :, sources:] = jnp.where(low, turned_r, xi).astype(bf16)
    xw_ref[1, :, :sources] = jnp.where(low, -xi, turned_r).astype(bf16)
    xw_ref[1, :, sources:] = jnp.where(low, -turned_i, xr).astype(bf16)
    v_loads[0].wait()
    value = jnp.dot(v_ref[0], xw_ref[0], preferred_element_type=f32)
    v_loads[1].wait()
    for load in loads[2:]:
        load.start()
    value = value + jnp.dot(v_ref[1], xw_ref[1], preferred_element_type=f32)
    for b in range(batches):
        rows_ref[b, pl.ds(0, total), :] = value[:, b * LANES : (b + 1) * LANES]
    loads[1].wait()
    row_start, column_start = 0, 0
    for k in range(n):
        start_ref[0, k] = row_start
        start_ref[1, k] = column_start
        row_start = row_start + rank_ref[me, k]
        column_start = column_start + rank_ref[k, me]
    pl.semaphore_wait(barrier, n - 1)
    for b in range(batches):
        send_rows(0, b, 1)

    for side in range(2):

        def entry(k, carry):
            tile, start = carry
            end = start + (rank_ref[me, tile] if side == 0 else rank_ref[tile, me])
            table_ref[side, 0, k] = jnp.clip(tile * RMAX + k * 8 - start, 0, n * RMAX)
            table_ref[side, 1, k] = jnp.clip((tile + 1) * RMAX + k * 8 - end, 0, n * RMAX)
            table_ref[side, 2, k] = end - k * 8
            leave = end <= k * 8 + 8
            later = jnp.minimum(tile + 1, n - 1)
            return jnp.where(leave, later, tile), jnp.where(leave, end, start)

        lax.fori_loop(0, blocks, entry, (jnp.int32(0), jnp.int32(0)))
    slots_ref[pl.ds(n * RMAX, 8), :] = jnp.zeros((8, LANES), f32)
    for p in range(2):
        turned = x_ref[p].T
        for b in range(batches):
            xt_ref[b, pl.ds(p * half, half), :] = turned[b * half : (b + 1) * half]
    for load in loads[2:]:
        load.wait()

    def field_of(b):
        c = joined_ref[...]
        p = dot_first(c, u_ref[0])
        q = dot_first(c, u_ref[1])
        yr = p[:half] - q[half:]
        yi = q[:half] + p[half:]
        rows = pl.ds(pl.multiple_of(b * half, half), half)
        hr = sums_ref[0, rows, :] * yr - sums_ref[1, rows, :] * yi - sums_ref[3, rows, :]
        hi = sums_ref[2, rows, :] * yi - sums_ref[1, rows, :] * yr + sums_ref[4, rows, :]
        return hr.astype(bf16), hi.astype(bf16)

    def step_model(b):
        a = joined_ref[...]
        p = dot_first(a, v_ref[0])
        q = dot_first(a, v_ref[1])
        xr = xt_ref[b, :half, :] - step_size * (p[:half] + q[half:])
        xi = xt_ref[b, half:, :] - step_size * (p[half:] - q[:half])
        return xr, xi

    for iteration in range(ITERS):
        e = 2 * iteration

        def residual_step(b, carry):
            if iteration == 0:
                first = b * half
                add_windows(record_ref, open_ref, close_ref, sums_ref, first, half)
            join(e, b, 0)
            hr, hi = field_of(b)
            rows_ref[b, pl.ds(0, total), :] = dot_last(
                u_ref[0], jnp.concatenate([hr, hi], axis=0)
            ) + dot_last(u_ref[1], jnp.concatenate([hi, -hr], axis=0))
            send_rows(e + 1, b, 0)
            return carry

        lax.fori_loop(0, batches, residual_step, 0)
        if iteration + 1 < ITERS:

            def model_step(b, carry):
                join(e + 1, b, 1)
                xr, xi = step_model(b)
                xt_ref[b, :half, :] = xr
                xt_ref[b, half:, :] = xi
                xr, xi = xr.astype(bf16), xi.astype(bf16)
                rows_ref[b, pl.ds(0, total), :] = dot_last(
                    v_ref[0], jnp.concatenate([xr, xi], axis=0)
                ) + dot_last(v_ref[1], jnp.concatenate([-xi, xr], axis=0))
                send_rows(e + 2, b, 1)
                return carry

            lax.fori_loop(0, batches, model_step, 0)
        else:
            for b in range(batches):
                join(e + 1, b, 1)
                xr, xi = step_model(b)
                out_ref[b, :half, :] = xr
                out_ref[b, half:, :] = xi

    def finish(e, carry):
        for b in range(batches):
            all_of(e, b).wait_send()
        return carry

    lax.fori_loop(0, 2 * ITERS, finish, 0)


def fused(start_model, v_basis, u_parts, records, ranks, window_start, window_stop):
    inputs = (ranks, start_model, v_basis, u_parts, records, window_start, window_stop)
    n = ranks.shape[0]
    _, width, sources = start_model.shape
    _, total, _ = v_basis.shape
    receivers = records.shape[2]
    exchanges, batches = 2 * ITERS, 2
    like = lambda a: pltpu.VMEM(a.shape, a.dtype)
    return pl.pallas_call(
        functools.partial(fused_kernel, n),
        out_shape=jax.ShapeDtypeStruct((batches, sources, width), f32),
        in_specs=[far] * 7,
        out_specs=near,
        scratch_shapes=[
            pltpu.SMEM(ranks.shape, ranks.dtype),
            like(start_model),
            like(v_basis),
            like(u_parts),
            like(records),
            like(window_start),
            like(window_stop),
            pltpu.VMEM((2, width, 2 * sources), bf16),
            pltpu.VMEM((batches, sources, width), f32),
            pltpu.VMEM((5, sources, receivers), f32),
            pltpu.VMEM((batches, total + RMAX, LANES), f32),
            pltpu.VMEM((n * RMAX + 8, LANES), f32),
            pltpu.VMEM((total, LANES), bf16),
            pltpu.VMEM((exchanges, batches, n - 1, RMAX, LANES), bf16),
            pltpu.VMEM((exchanges, batches, n, RMAX, LANES), bf16),
            pltpu.SMEM((2, n), jnp.int32),
            pltpu.SMEM((2, 3, total // 8), jnp.int32),
            pltpu.SemaphoreType.DMA((6,)),
            pltpu.SemaphoreType.DMA((2,)),
            pltpu.SemaphoreType.DMA((exchanges, batches)),
            pltpu.SemaphoreType.DMA((exchanges, batches)),
        ],
        compiler_params=pltpu.CompilerParams(
            collective_id=0, has_side_effects=True, vmem_limit_bytes=44 * 1024 * 1024
        ),
    )(*[pltpu.with_memory_space_constraint(a, pltpu.HBM) for a in inputs])


def turn_kernel(xt_ref, out_ref):
    batches, sources, _ = xt_ref.shape
    half = sources // batches
    rows = pl.ds(pl.multiple_of(pl.program_id(0) * half, half), half)
    part = [xt_ref[b, rows, :] for b in range(batches)]
    out_ref[0] = jnp.concatenate(part, axis=0).T


def by_row(xt):
    _, sources, width = xt.shape
    return pl.pallas_call(
        turn_kernel,
        grid=(2,),
        out_shape=jax.ShapeDtypeStruct((2, width, sources), xt.dtype),
        in_specs=[near],
        out_specs=pl.BlockSpec((1, width, sources), lambda p: (p, 0, 0)),
        compiler_params=pltpu.CompilerParams(vmem_limit_bytes=16 * 1024 * 1024),
    )(xt)


def on_device(start_model, v_basis, u_basis, records, tile_ranks, window_start, window_stop):
    n = lax.axis_size("tile")
    freq_count, rows_count, cols_count = tile_ranks.shape
    single = freq_count == 1 and n == rows_count and n == cols_count and n >= 4 and n & (n - 1) == 0
    fits = start_model.shape[2] == LANES and v_basis.shape[1] % 16 == 0
    fits = fits and records.shape[2] % (4 * LANES) == 0 and start_model.shape[1] % LANES == 0
    if not (single and fits):
        return on_device_general(
            start_model, v_basis, u_basis, records, tile_ranks, window_start, window_stop
        )
    xt = fused(
        start_model, v_basis, u_basis[:, 0], records, tile_ranks[0], window_start, window_stop
    )
    return by_row(xt)


def solution(mesh):
    in_specs = (
        P(None, ("groups", "tile"), None),
        P(None, ("groups", "tile"), None),
        P(None, None, None, ("groups", "tile")),
        P(None, None, ("groups", "tile")),
        P("groups", None, None),
        P(None, ("groups", "tile")),
        P(None, ("groups", "tile")),
    )
    out_specs = P(None, ("groups", "tile"), None)
    return jax.shard_map(
        on_device, mesh=mesh, in_specs=in_specs, out_specs=out_specs, check_vma=False
    )
```
